32 devices in a mesh: groups: 2 (over y), ctx: 4 (over z), chan: 4 (over x, core).
Axes of the slice: x: 2, y: 2, z: 4, core: 2. Of those that a mesh axis runs over, the one named last changes fastest.
Arguments:
- q_feat: bfloat16 [4096, 8192], P(('groups', 'ctx'), 'chan'), parts along dimension 0, may hold values from -6 to 6
- k_feat: bfloat16 [4096, 8192], P(('groups', 'ctx'), 'chan'), parts along dimension 0, may hold values from -6 to 6
- v_feat: bfloat16 [4096, 8192], P(('groups', 'ctx'), 'chan'), parts along dimension 0, may hold values from -6 to 6
- pole_rate: float32 [16, 8192], P(None, 'chan'), may hold values from 4.8828126e-05 to 0.03
- residue: float32 [16, 8192], P(None, 'chan'), may hold values from -1.5 to 1.5
- skip_gain: float32 [8192], P('chan'), may hold values from 0.5 to 1.5
- lengths: int32 [8], P('groups'), parts along dimension 0, may hold values from 1 to 1024, 2048 in all
- owners: int32 [8], P('groups'), parts along dimension 0, may hold values from 0 to 3, as said below
Outputs:
- mixed_out: bfloat16 [4096, 8192], P(('groups', 'ctx'), 'chan'), parts along dimension 0
- decode_state: float32 [8, 16, 8192], P(('groups', 'ctx'), None, 'chan'), parts along dimension 0
The draws below stay inside these ranges and needn't reach their ends.
There are 2 independent parts, one for each index of `groups`. The reference program is written for one: setup_inputs(seed, part) draws one part's arguments, and reference() takes and returns one part's arrays. A program takes and returns all parts, laid end to end along the dimension named above; an argument that names none is the same for every part. Nothing has to cross between parts.
Inputs may be any that keep to these rules, and one draw needn't show every extreme that they name: The 4 lengths sum to 2048; the longest is exactly 1024. The 4 owners are distinct.
All inputs are finite; a program needn't handle non-finite values.
Results may differ from the reference program's by a relative error of at most 0.001.
Values sent between devices are 32-bit elements; how exact they have to be, the bound alone decides.
A program may use at most 128 MiB of HBM per device.

```python
import math
import jax
import jax.numpy as jnp
import numpy as np
from jax import lax

D = 8192
POLES = 16
REQS = 4
TOKENS = 2048
OWNER_SLOTS = 4
N_CTX = 4


def draw_owners(key, part):
    middle = 1 + jax.random.permutation(jax.random.fold_in(key, 17), N_CTX - 2)[:REQS - 2]
    values = jnp.concatenate([jnp.array([N_CTX - 1, 0], jnp.int32), middle.astype(jnp.int32)])
    order = jax.random.permutation(jax.random.fold_in(key, 23), REQS)
    return values[order].astype(jnp.int32)


def block_levels(rng, dims, shards, smallest, top_value):
    factor_of, own = 1.0, jax.random.fold_in(rng, 6)
    for dim, parts in shards:
        draws = jnp.exp(jax.random.uniform(jax.random.fold_in(own, dim), (parts,), jnp.float32, smallest / len(shards), top_value / len(shards)))
        factor_of = factor_of * jnp.repeat(draws, dims[dim] // parts).reshape([-1 if axis == dim else 1 for axis in range(len(dims))])
    return factor_of


def length_profile(amount, total, most, slope):
    loads = [(1 << 20) // math.isqrt(standing ** slope) + 1 for standing in range(2, amount + 1)]
    spare, holding = total - most - (amount - 1), [1] * (amount - 1)
    while spare > 0:
        free = [i for i in range(amount - 1) if holding[i] < most]
        whole, remaining = sum([loads[i] for i in free]), spare
        for i in free:
            more = min(most - holding[i], max(1, remaining * loads[i] // whole), spare)
            holding[i] = holding[i] + more
            spare = spare - more
    return np.array([most] + holding)


def ragged_sizes(stream_key, number_of, total, most, lean):
    if number_of == 2:
        one = jax.random.randint(stream_key, (), max(1, total - most), min(most, total - 1) + 1)
        return jnp.stack([one, total - one])
    sizes = jnp.asarray(length_profile(number_of, total, most, lean), jnp.int32)
    twos = (number_of - 1) // 2
    giver, receiver = sizes[1:1 + 2 * twos:2], sizes[2:2 + 2 * twos:2]
    margin = jnp.minimum(giver - 1, most - receiver)
    moved = jax.random.randint(jax.random.fold_in(stream_key, 1), (twos,), 0, 1 << 20) % (margin + 1)
    sizes = sizes.at[1:1 + 2 * twos:2].set(giver - moved).at[2:2 + 2 * twos:2].set(receiver + moved)
    return sizes[jax.random.permutation(jax.random.fold_in(stream_key, 2), number_of)]


def centred(rng, extent, width, most, pieces=(), held_as=jnp.bfloat16):
    values = width * jax.random.normal(rng, extent, jnp.float32)
    if pieces:
        values = values * block_levels(rng, extent, pieces, -0.22, 0.18)
    return jnp.clip(values, -most, most).astype(held_as)


def setup_inputs(seed: int = 0, part: int = 0) -> dict:
    splits = jax.random.split(jax.random.key(seed), 9)
    part_splits = jax.random.split(jax.random.fold_in(splits[8], part), 9)
    q_feat = centred(part_splits[0], (TOKENS, D), 1.0, 6.0, ((0, 4), (1, 4)))
    k_feat = centred(part_splits[1], (TOKENS, D), 1.0, 6.0, ((0, 4), (1, 4)))
    v_feat = centred(part_splits[2], (TOKENS, D), 1.0, 6.0, ((0, 4), (1, 4)))
    pole_rate = jnp.clip(jnp.exp(math.log(0.03) - 6.420646 * jax.random.uniform(splits[3], (POLES, D), jnp.float32) ** block_levels(splits[3], (POLES, D), ((1, 4),), -0.2, 0.2)), 4.882812572759576e-05, 0.03)
    residue = centred(splits[4], (POLES, D), 0.25, 1.5, ((1, 4),), jnp.float32)
    skip_gain = jnp.clip(0.5 + 1.0 * jax.random.uniform(splits[5], (D,), jnp.float32) ** block_levels(splits[5], (D,), ((0, 4),), -0.2, 0.2), 0.5, 1.5)
    lengths = ragged_sizes(part_splits[6], REQS, TOKENS, TOKENS // 2, 2).astype(jnp.int32)
    owners = draw_owners(jax.random.fold_in(jax.random.fold_in(splits[8], part), 71), part)
    return dict(q_feat=q_feat, k_feat=k_feat, v_feat=v_feat, pole_rate=pole_rate, residue=residue, skip_gain=skip_gain, lengths=lengths, owners=owners)


def reference(q_feat, k_feat, v_feat, pole_rate, residue, skip_gain, lengths, owners):
    mixed_in = k_feat.astype(jnp.float32) * v_feat.astype(jnp.float32)
    offsets = (jnp.cumsum(lengths) - lengths).astype(jnp.int32)
    positions = jnp.arange(TOKENS, dtype=jnp.int32)
    segment = (lax.optimization_barrier(jnp.sum((positions[:, None] >= offsets[None, :]).astype(jnp.int32), axis=1)) - 1).astype(jnp.int32)
    is_start = positions == offsets[segment]
    pole_decay = jnp.exp(-pole_rate)
    scaled_res = residue * jnp.sqrt(1.0 - jnp.exp(-2.0 * pole_rate))

    def advance(loop_carry, inputs_now):
        mode_state, store = loop_carry
        row_in, seg_now, start_now = inputs_now
        mode_state = jnp.where(start_now, jnp.zeros_like(mode_state), pole_decay * mode_state) + row_in[None, :]
        store = store.at[seg_now].set(mode_state)
        return ((mode_state, store), lax.optimization_barrier(jnp.sum(scaled_res * mode_state, axis=0)))
    init_state = jnp.zeros((POLES, D), jnp.float32)
    init_store = jnp.zeros((REQS, POLES, D), jnp.float32)
    (last_state, store), conv = lax.scan(advance, (init_state, init_store), (mixed_in, segment, is_start))
    mixed_out = (q_feat.astype(jnp.float32) * (conv + skip_gain[None, :] * mixed_in)).astype(jnp.bfloat16)
    decode_state = jnp.zeros((OWNER_SLOTS, POLES, D), jnp.float32).at[owners.astype(jnp.int32)].set(store)
    return (mixed_out, decode_state)
```

```python
import functools

import jax
import jax.numpy as jnp
from jax import lax
from jax.experimental import pallas as pl
from jax.experimental.pallas import tpu as pltpu
from jax.sharding import PartitionSpec as P

F32 = jnp.float32
LANES = 128
ROWS = 8
MESH = pl.DeviceIdType.MESH


def lane(c):
    if isinstance(c, int):
        return pl.ds(c * LANES, LANES)
    return pl.ds(pl.multiple_of(c * LANES, LANES), LANES)


def kernel(
    lens_ref, own_ref, rate_hbm, res_hbm, gain_hbm, k_hbm, v_hbm, q_hbm,
    out_ref, dec_ref,
    k_ref, v_ref, q_ref, rate_ref, res_ref, gain_ref, u_ref, um_ref, s_ref, w_ref,
    dtab, etab, ftab, cs_ref, mtab, fix_ref, tbuf,
    arrived, passed, arr_r, put_r, arr_l, put_l,
    where_ref, kind_ref, inside_ref, par_sem, kv_sem, q_sem, st_send, st_recv, r_send, r_recv, l_send, l_recv,
    *, tok, poles, count, cols, per,
):
    slots = lax.axis_size("ctx")
    last = slots - 1
    me = lax.axis_index("ctx")
    tiles = cols // per
    halves = poles // ROWS
    chunks = tok // ROWS
    width = per * LANES
    barrier = pltpu.get_barrier_semaphore()

    @pl.when(me > 0)
    def _():
        pl.semaphore_signal(barrier, inc=1, device_id={"ctx": me - 1}, device_id_type=MESH)

    @pl.when(me < last)
    def _():
        pl.semaphore_signal(barrier, inc=1, device_id={"ctx": me + 1}, device_id_type=MESH)

    params = [
        pltpu.make_async_copy(src, dst, par_sem.at[i])
        for i, (src, dst) in enumerate(
            [(rate_hbm, rate_ref), (res_hbm, res_ref), (gain_hbm, gain_ref)]
        )
    ]
    params[0].start()
    loads = []
    for t in range(tiles):
        at = pl.ds(t * width, width)
        loads.append(
            [
                pltpu.make_async_copy(src.at[:, at], dst.at[:, at], kv_sem.at[t, i])
                for i, (src, dst) in enumerate([(k_hbm, k_ref), (v_hbm, v_ref)])
            ]
        )
        for copy in loads[t]:
            copy.start()
    params[1].start()
    params[2].start()
    q_load = pltpu.make_async_copy(q_hbm, q_ref, q_sem)
    q_load.start()

    first = me * tok
    offset = jnp.int32(0)
    begin, final = [], []
    for r in range(count):
        begin.append(offset - first)
        offset = offset + lens_ref[r]
        final.append(offset - 1 - first)
    starts = begin[1:]
    inner = len(starts)
    zero_row = count + 1

    where_in = [lax.shift_right_arithmetic(a, 3) for a in starts]
    rel_in = [lax.bitwise_and(a, ROWS - 1) for a in starts]

    def last_in(n):
        found = jnp.int32(-1)
        for chunk, rel in zip(where_in, rel_in):
            found = jnp.maximum(found, jnp.where(chunk == n, rel, -1))
        return found

    def first_in(n):
        found = jnp.int32(ROWS)
        for chunk, rel in zip(where_in, rel_in):
            found = jnp.minimum(found, jnp.where(chunk == n, rel, ROWS))
        return found

    def keeps(n):
        hit = jnp.int32(1)
        for chunk in where_in:
            hit = jnp.where(chunk == n, 0, hit)
        return hit

    covers = jnp.int32(1)
    ends_here, goes_on = [], []
    dist = jnp.int32(0)
    for a in starts:
        covers = jnp.where((a >= 0) & (a < tok), 0, covers)
    for r in range(count):
        ends_here.append((final[r] >= 0) & (final[r] < tok))
        goes_on.append((begin[r] < tok) & (final[r] >= tok))
        dist = jnp.where(goes_on[r], final[r] - (tok - 1), dist)

    def source_of(slot):
        row = jnp.int32(zero_row)
        for r in range(count):
            kind = jnp.where(ends_here[r], r, jnp.where(goes_on[r], count, zero_row))
            row = jnp.where(own_ref[r] == slot, kind, row)
        return row

    iota = lax.broadcasted_iota(jnp.int32, (ROWS, LANES), 0)

    def bcast(row):
        return jnp.broadcast_to(row, (ROWS, LANES))

    for n in range(ROWS + 1):
        mtab[n] = (iota < n).astype(F32)
    fix_ref[inner] = jnp.zeros((ROWS, LANES), F32)
    tbuf[zero_row] = jnp.zeros(tbuf.shape[1:], F32)
    dtab[0] = jnp.zeros(dtab.shape[1:], F32)
    dtab[2] = jnp.ones(dtab.shape[1:], F32)
    etab[0] = jnp.zeros(etab.shape[1:], F32)
    ftab[0] = jnp.zeros(ftab.shape[1:], F32)
    params[0].wait()
    rate = rate_ref[...]
    dtab[1] = jnp.exp(-rate)
    etab[1] = jnp.exp(rate * -float(ROWS))
    ftab[1] = jnp.exp(rate * -float(tok))
    ftab[2] = jnp.exp(rate * -dist.astype(F32))

    def part(h):
        return pl.ds(h * ROWS, ROWS)

    def mix(t):
        def body(m, _):
            for half in range(2):
                n = 4 * m + 2 * half
                rows = pl.ds(pl.multiple_of(n * ROWS, 2 * ROWS), 2 * ROWS)
                masks = [iota >= last_in(n + i) for i in range(2)]
                for c in range(t * per, (t + 1) * per):
                    u = k_ref[rows, lane(c)].astype(F32) * v_ref[rows, lane(c)].astype(F32)
                    u_ref[c, rows, :] = u
                    for i in range(2):
                        at = pl.ds(pl.multiple_of((n + i) * ROWS, ROWS), ROWS)
                        um_ref[c, at, :] = jnp.where(
                            masks[i], u[i * ROWS : (i + 1) * ROWS], 0.0
                        )
            return 0

        lax.fori_loop(0, chunks // 4, body, 0)

    def scan(t):
        pairs = [(c, h) for c in range(t * per, (t + 1) * per) for h in range(halves)]

        def body(m, state):
            state = list(state)
            for i in range(4):
                n = 4 * m + i
                base = n * ROWS
                keep = keeps(n)
                for x, (c, h) in enumerate(pairs):
                    s_ref[c, n, part(h), :] = state[x]
                local = [None] * len(pairs)
                for j in range(ROWS):
                    rows = {
                        c: bcast(um_ref[c, pl.ds(base + j, 1), :])
                        for c in range(t * per, (t + 1) * per)
                    }
                    for x, (c, h) in enumerate(pairs):
                        if j == 0:
                            local[x] = rows[c]
                        else:
                            local[x] = dtab[1, part(h), lane(c)] * local[x] + rows[c]
                for x, (c, h) in enumerate(pairs):
                    state[x] = etab[keep, part(h), lane(c)] * state[x] + local[x]
            return tuple(state)

        zero = jnp.zeros((ROWS, LANES), F32)
        state = lax.fori_loop(0, chunks // 4, body, tuple(zero for _ in pairs))
        for x, (c, h) in enumerate(pairs):
            s_ref[c, chunks, part(h), :] = state[x]
            tbuf[count, part(h), lane(c)] = state[x] * ftab[2, part(h), lane(c)]

            @pl.when(me == 0)
            def _():
                passed[part(h), lane(c)] = state[x]

    for r in range(count):
        end = jnp.clip(final[r], 0, tok - 1)
        n = lax.shift_right_logical(end, 3)
        stop = end - n * ROWS
        b = begin[r] - n * ROWS
        where_ref[r] = n
        for j in range(ROWS):
            kind = jnp.where(j > stop, 2, jnp.where(j <= b, 0, 1))
            kind_ref[r, j] = jnp.where(ends_here[r], kind, 0)
            inside = ends_here[r] & (j >= b) & (j <= stop)
            inside_ref[r, j] = jnp.where(inside, 1.0, 0.0).astype(F32)

    def tails(t):
        for r in range(count):
            n = where_ref[r]
            kinds = [kind_ref[r, j] for j in range(ROWS)]
            weights = [inside_ref[r, j] for j in range(ROWS)]
            for c in range(t * per, (t + 1) * per):
                value = [s_ref[c, n, part(h), :] for h in range(halves)]
                for j in range(ROWS):
                    row = bcast(u_ref[c, pl.ds(n * ROWS + j, 1), :]) * weights[j]
                    value = [
                        dtab[kinds[j], part(h), lane(c)] * x + row for h, x in enumerate(value)
                    ]
                for h in range(halves):
                    tbuf[r, part(h), lane(c)] = value[h]

    def span(t):
        return pl.ds(t * width, width)

    def pass_on(t):
        return pltpu.make_async_remote_copy(
            src_ref=passed.at[:, span(t)], dst_ref=arrived.at[:, span(t)],
            send_sem=st_send.at[t], recv_sem=st_recv.at[t],
            device_id={"ctx": me + 1}, device_id_type=MESH,
        )

    def arrival(t):
        return pltpu.make_async_remote_copy(
            src_ref=passed.at[:, span(t)], dst_ref=arrived.at[:, span(t)],
            send_sem=st_send.at[t], recv_sem=st_recv.at[t],
            device_id={"ctx": me - 1}, device_id_type=MESH,
        )

    def relay(t):
        arrival(t).wait_recv()

        @pl.when(me < last)
        def _():
            for c in range(t * per, (t + 1) * per):
                for h in range(halves):
                    passed[part(h), lane(c)] = (
                        s_ref[c, chunks, part(h), :]
                        + ftab[covers, part(h), lane(c)] * arrived[part(h), lane(c)]
                    )
            pass_on(t).start()

    def to_right(i, t):
        return pltpu.make_async_remote_copy(
            src_ref=put_r.at[i, :, span(t)], dst_ref=arr_r.at[i, :, span(t)],
            send_sem=r_send.at[i, t], recv_sem=r_recv.at[i, t],
            device_id={"ctx": me + 1}, device_id_type=MESH,
        )

    def to_left(i, t):
        return pltpu.make_async_remote_copy(
            src_ref=put_l.at[i, :, span(t)], dst_ref=arr_l.at[i, :, span(t)],
            send_sem=l_send.at[i, t], recv_sem=l_recv.at[i, t],
            device_id={"ctx": me - 1}, device_id_type=MESH,
        )

    back = last - me

    def hop(i, t):
        at = span(t)

        @pl.when((me <= i) & (me < last))
        def _():
            own = tbuf[source_of(me + last - i), :, at]
            put_r[i, :, at] = own
            if i:

                @pl.when(me > 0)
                def _():
                    to_right(i - 1, t).wait_recv()
                    put_r[i, :, at] = own + arr_r[i - 1, :, at]

            to_right(i, t).start()

        @pl.when((back <= i) & (back < last))
        def _():
            own = tbuf[source_of(i - back), :, at]
            put_l[i, :, at] = own
            if i:

                @pl.when(back > 0)
                def _():
                    to_left(i - 1, t).wait_recv()
                    put_l[i, :, at] = own + arr_l[i - 1, :, at]

            to_left(i, t).start()

    hops = last
    points = 2 * tiles
    lag = 2

    def serve(point):
        for t in range(tiles):
            if point < points:
                due = (me > 0) & (t + lag * me == point)
            elif t == point - points:
                due = (me > 0) & (t + lag * me >= points)
            else:
                continue

            @pl.when(due)
            def _():
                relay(t)

    def taps(c):
        at = lane(c)
        steps = (iota + 1).astype(F32)
        total = jnp.zeros((ROWS, LANES), F32)
        head = bcast(gain_ref[0:1, at])
        for p in range(poles):
            scale = bcast(cs_ref[pl.ds(p, 1), at])
            value = scale * jnp.exp(bcast(rate_ref[pl.ds(p, 1), at]) * -steps)
            w_ref[c, p] = value
            total = total + value
            head = head + scale
        lead = jnp.where(iota == 0, head, pltpu.roll(total, 1, 0))
        taps = [lead] + [
            jnp.where(iota >= j, pltpu.roll(lead, j, 0), 0.0) for j in range(1, ROWS)
        ]
        for x, a in enumerate(starts):
            base = lax.shift_right_logical(jnp.clip(a, 0, tok - 1), 3) * ROWS
            value = jnp.zeros((ROWS, LANES), F32)
            for j in range(ROWS - 1):
                cut = jnp.int32(ROWS)
                for other in starts:
                    rel = other - base
                    cut = jnp.minimum(cut, jnp.where(rel > j, rel, ROWS))
                row = bcast(u_ref[c, pl.ds(base + j, 1), :])
                value = value - jnp.where(iota >= cut, taps[j], 0.0) * row
            fix_ref[x] = value

        def body(m, _):
            for i in range(4):
                n = m * 4 + i
                which = jnp.int32(inner)
                for x, chunk in enumerate(where_in):
                    which = jnp.where(chunk == n, x, which)
                acc = [fix_ref[which], None]
                for j in range(ROWS):
                    term = taps[j] * bcast(u_ref[c, pl.ds(n * ROWS + j, 1), :])
                    acc[j % 2] = term if acc[j % 2] is None else acc[j % 2] + term
                um_ref[c, pl.ds(pl.multiple_of(n * ROWS, ROWS), ROWS), :] = acc[0] + acc[1]
            return 0

        lax.fori_loop(0, chunks // 4, body, 0)

    def carry(t):
        pairs = [(c, h) for c in range(t * per, (t + 1) * per) for h in range(halves)]

        def body(m, state):
            state = list(state)
            for i in range(4):
                n = m * 4 + i
                keep = keeps(n)
                for x, (c, h) in enumerate(pairs):
                    s_ref[c, n, part(h), :] = s_ref[c, n, part(h), :] + state[x]
                    state[x] = etab[keep, part(h), lane(c)] * state[x]
            return tuple(state)

        lax.fori_loop(
            0, chunks // 4, body, tuple(arrived[part(h), lane(c)] for c, h in pairs)
        )

    def emit(c):
        at = lane(c)
        weight = [w_ref[c, p] for p in range(poles)]

        def body(m, _):
            for half in range(2):
                rows = pl.ds(pl.multiple_of((2 * m + half) * 2 * ROWS, 2 * ROWS), 2 * ROWS)
                near = um_ref[c, rows, :]
                made = []
                for i in range(2):
                    n = 4 * m + 2 * half + i
                    acc = [None] * 4
                    for p in range(poles):
                        term = weight[p] * bcast(s_ref[c, n, pl.ds(p, 1), :])
                        acc[p % 4] = term if acc[p % 4] is None else acc[p % 4] + term
                    total = (acc[0] + acc[1]) + (acc[2] + acc[3])
                    made.append(near[i * ROWS : (i + 1) * ROWS] + mtab[first_in(n)] * total)
                y = jnp.concatenate(made, axis=0)
                out_ref[rows, at] = (q_ref[rows, at].astype(F32) * y).astype(out_ref.dtype)
            return 0

        lax.fori_loop(0, chunks // 4, body, 0)

    for t in range(tiles):
        for copy in loads[t]:
            copy.wait()
        mix(t)
        scan(t)
        if t == 0:
            near = (me > 0).astype(jnp.int32) + (me < last).astype(jnp.int32)
            pl.semaphore_wait(barrier, near)

        @pl.when((me == 0) & (me < last))
        def _():
            pass_on(t).start()

        tails(t)
        hop(0, t)
        serve(t)

    params[1].wait()
    params[2].wait()
    cs_ref[...] = res_ref[...] * jnp.sqrt(1.0 - jnp.exp(-2.0 * rate_ref[...]))
    for t in range(tiles):

        def one(c, _):
            taps(c)
            return 0

        lax.fori_loop(t * per, (t + 1) * per, one, 0)
        if hops > 1:
            hop(1, t)
        serve(tiles + t)

    q_load.wait()
    todo = [(i, t) for i in range(2, hops) for t in range(tiles)]
    for t in range(tiles):
        serve(points + t)

        @pl.when(me > 0)
        def _():
            carry(t)

        for g in range(0, per, 2):
            size = min(2, per - g)

            def one(c, _):
                emit(c)
                return 0

            lax.fori_loop(t * per + g, t * per + g + size, one, 0)
            if t * per + g >= cols // 4 and todo:
                hop(*todo.pop(0))
    for item in todo:
        hop(*item)

    dec_ref[0] = tbuf[source_of(me), :, :]
    for t in range(tiles):
        at = span(t)

        @pl.when(me > 0)
        def _():
            to_right(hops - 1, t).wait_recv()
            dec_ref[0, :, at] = dec_ref[0, :, at] + arr_r[hops - 1, :, at]

        @pl.when(me < last)
        def _():
            to_left(hops - 1, t).wait_recv()
            dec_ref[0, :, at] = dec_ref[0, :, at] + arr_l[hops - 1, :, at]

    for t in range(tiles):

        @pl.when(me < last)
        def _():
            pass_on(t).wait_send()

        for i in range(hops):

            @pl.when((me <= i) & (me < last))
            def _():
                to_right(i, t).wait_send()

            @pl.when((back <= i) & (back < last))
            def _():
                to_left(i, t).wait_send()


def shards(q_feat, k_feat, v_feat, pole_rate, residue, skip_gain, lengths, owners):
    tok, channels = q_feat.shape
    poles, count = pole_rate.shape[0], lengths.shape[0]
    slots = lax.axis_size("ctx")
    cols = channels // LANES
    per = min(4, cols)
    tiles = cols // per
    chunks = tok // ROWS
    hops = max(slots - 1, 1)
    dma = pltpu.SemaphoreType.DMA
    vmem, hbm = pl.BlockSpec(memory_space=pltpu.VMEM), pl.BlockSpec(memory_space=pltpu.HBM)
    smem = pl.BlockSpec(memory_space=pltpu.SMEM)
    state = pltpu.VMEM((poles, channels), F32)
    block = pltpu.VMEM((hops, poles, channels), F32)
    feat = pltpu.VMEM((tok, channels), q_feat.dtype)
    wide = pltpu.VMEM((cols, tok, LANES), F32)
    far = [
        pltpu.with_memory_space_constraint(x, pltpu.HBM)
        for x in (pole_rate, residue, skip_gain[None, :], k_feat, v_feat, q_feat)
    ]
    return pl.pallas_call(
        functools.partial(kernel, tok=tok, poles=poles, count=count, cols=cols, per=per),
        in_specs=[smem] * 2 + [hbm] * 6,
        out_specs=[vmem, vmem],
        out_shape=[
            jax.ShapeDtypeStruct((tok, channels), q_feat.dtype),
            jax.ShapeDtypeStruct((1, poles, channels), F32),
        ],
        scratch_shapes=[
            feat, feat, feat, state, state, pltpu.VMEM((1, channels), F32), wide, wide,
            pltpu.VMEM((cols, chunks + 1, poles, LANES), F32),
            pltpu.VMEM((cols, poles, ROWS, LANES), F32),
            pltpu.VMEM((3, poles, channels), F32),
            pltpu.VMEM((2, poles, channels), F32),
            pltpu.VMEM((3, poles, channels), F32),
            state,
            pltpu.VMEM((ROWS + 1, ROWS, LANES), F32),
            pltpu.VMEM((count, ROWS, LANES), F32),
            pltpu.VMEM((count + 2, poles, channels), F32),
            state, state, block, block, block, block,
            pltpu.SMEM((count,), jnp.int32), pltpu.SMEM((count, ROWS), jnp.int32),
            pltpu.SMEM((count, ROWS), F32),
            dma((3,)), dma((tiles, 2)), dma, dma((tiles,)), dma((tiles,)),
            dma((hops, tiles)), dma((hops, tiles)), dma((hops, tiles)), dma((hops, tiles)),
        ],
        compiler_params=pltpu.CompilerParams(
            collective_id=0, has_side_effects=True, vmem_limit_bytes=40 << 20
        ),
        name="modal",
    )(lengths, owners, *far)


def solution(mesh):
    tokens = P(("groups", "ctx"), "chan")
    return jax.shard_map(
        shards,
        mesh=mesh,
        in_specs=(
            tokens, tokens, tokens, P(None, "chan"), P(None, "chan"), P("chan"),
            P("groups"), P("groups"),
        ),
        out_specs=(tokens, P(("groups", "ctx"), None, "chan")),
        check_vma=False,
    )
```

```python
import functools

import jax
import jax.numpy as jnp
from jax import lax
from jax.experimental import pallas as pl
from jax.experimental.pallas import tpu as pltpu
from jax.sharding import PartitionSpec as P

F32 = jnp.float32
LANES = 128
ROWS = 8
MIX, SCAN, FIR, CARRY, EMIT = 8, 8, 16, 8, 16
MESH = pl.DeviceIdType.MESH


def lane(c):
    if isinstance(c, int):
        return pl.ds(c * LANES, LANES)
    return pl.ds(pl.multiple_of(c * LANES, LANES), LANES)


def kernel(
    lens_hbm, own_hbm, rate_hbm, res_hbm, gain_hbm, k_hbm, v_hbm, q_hbm,
    out_ref, dec_ref,
    lens_ref, own_ref, k_ref, v_ref, q_ref, rate_ref, res_ref, gain_ref, u_ref, um_ref, s_ref, w_ref,
    dtab, etab, ftab, cs_ref, mtab, ltab, fix_ref, tbuf,
    arrived, passed, arr_r, put_r, arr_l, put_l,
    which_ref, where_ref, kind_ref, inside_ref, par_sem, kv_sem, q_sem, st_send, st_recv, r_send, r_recv, l_send, l_recv,
    *, tok, poles, count, cols, per,
):
    slots = lax.axis_size("ctx")
    last = slots - 1
    me = lax.axis_index("ctx")
    tiles = cols // per
    halves = poles // ROWS
    chunks = tok // ROWS
    width = per * LANES
    barrier = pltpu.get_barrier_semaphore()

    @pl.when(me > 0)
    def _():
        pl.semaphore_signal(barrier, inc=1, device_id={"ctx": me - 1}, device_id_type=MESH)

    @pl.when(me < last)
    def _():
        pl.semaphore_signal(barrier, inc=1, device_id={"ctx": me + 1}, device_id_type=MESH)

    params = [
        pltpu.make_async_copy(src, dst, par_sem.at[i])
        for i, (src, dst) in enumerate(
            [
                (rate_hbm, rate_ref), (res_hbm, res_ref), (gain_hbm, gain_ref),
                (lens_hbm, lens_ref), (own_hbm, own_ref),
            ]
        )
    ]
    for i in (3, 4, 0):
        params[i].start()
    loads = []
    for t in range(tiles):
        at = pl.ds(t * width, width)
        loads.append(
            [
                pltpu.make_async_copy(src.at[:, at], dst.at[:, at], kv_sem.at[t, i])
                for i, (src, dst) in enumerate([(k_hbm, k_ref), (v_hbm, v_ref)])
            ]
        )
        for copy in loads[t]:
            copy.start()
    params[1].start()
    params[2].start()
    q_load = pltpu.make_async_copy(q_hbm, q_ref, q_sem)
    q_load.start()

    params[3].wait()
    params[4].wait()
    first = me * tok
    offset = jnp.int32(0)
    begin, final = [], []
    for r in range(count):
        begin.append(offset - first)
        offset = offset + lens_ref[r]
        final.append(offset - 1 - first)
    starts = begin[1:]
    inner = len(starts)
    zero_row = count + 1

    where_in = [lax.shift_right_arithmetic(a, 3) for a in starts]
    rel_in = [lax.bitwise_and(a, ROWS - 1) for a in starts]

    def mark(m, _):
        for i in range(4):
            n = m * 4 + i
            which = jnp.int32(inner)
            for x, chunk in enumerate(where_in):
                which = jnp.where(chunk == n, x, which)
            which_ref[n] = which
        return 0

    lax.fori_loop(0, chunks // 4, mark, 0)

    covers = jnp.int32(1)
    ends_here, goes_on = [], []
    dist = jnp.int32(0)
    for a in starts:
        covers = jnp.where((a >= 0) & (a < tok), 0, covers)
    for r in range(count):
        ends_here.append((final[r] >= 0) & (final[r] < tok))
        goes_on.append((begin[r] < tok) & (final[r] >= tok))
        dist = jnp.where(goes_on[r], final[r] - (tok - 1), dist)

    def source_of(slot):
        row = jnp.int32(zero_row)
        for r in range(count):
            kind = jnp.where(ends_here[r], r, jnp.where(goes_on[r], count, zero_row))
            row = jnp.where(own_ref[r] == slot, kind, row)
        return row

    iota = lax.broadcasted_iota(jnp.int32, (ROWS, LANES), 0)

    def bcast(row):
        return jnp.broadcast_to(row, (ROWS, LANES))

    mtab[inner] = jnp.ones((ROWS, LANES), F32)
    ltab[inner] = jnp.ones((ROWS, LANES), F32)
    for x, chunk in enumerate(where_in):
        low, high = jnp.int32(ROWS), jnp.int32(-1)
        for other, rel in zip(where_in, rel_in):
            low = jnp.where(other == chunk, jnp.minimum(low, rel), low)
            high = jnp.where(other == chunk, jnp.maximum(high, rel), high)
        mtab[x] = jnp.where(iota < low, 1.0, 0.0)
        ltab[x] = jnp.where(iota >= high, 1.0, 0.0)
    fix_ref[inner] = jnp.zeros((ROWS, LANES), F32)
    tbuf[zero_row] = jnp.zeros(tbuf.shape[1:], F32)
    dtab[0] = jnp.zeros(dtab.shape[1:], F32)
    dtab[2] = jnp.ones(dtab.shape[1:], F32)
    for x in range(inner):
        etab[x] = jnp.zeros(etab.shape[1:], F32)
    ftab[0] = jnp.zeros(ftab.shape[1:], F32)
    params[0].wait()
    rate = rate_ref[...]
    dtab[1] = jnp.exp(-rate)
    etab[inner] = jnp.exp(rate * -float(ROWS))
    ftab[1] = jnp.exp(rate * -float(tok))
    ftab[2] = jnp.exp(rate * -dist.astype(F32))

    def part(h):
        return pl.ds(h * ROWS, ROWS)

    def mix(t):
        def body(m, _):
            for half in range(MIX // 2):
                n = MIX * m + 2 * half
                rows = pl.ds(pl.multiple_of(n * ROWS, 2 * ROWS), 2 * ROWS)
                masks = [ltab[which_ref[n + i]] for i in range(2)]
                for c in range(t * per, (t + 1) * per):
                    u = k_ref[rows, lane(c)].astype(F32) * v_ref[rows, lane(c)].astype(F32)
                    u_ref[c, rows, :] = u
                    for i in range(2):
                        at = pl.ds(pl.multiple_of((n + i) * ROWS, ROWS), ROWS)
                        um_ref[c, at, :] = u[i * ROWS : (i + 1) * ROWS] * masks[i]
            return 0

        lax.fori_loop(0, chunks // MIX, body, 0)

    def scan(t):
        pairs = [(c, h) for c in range(t * per, (t + 1) * per) for h in range(halves)]

        def body(m, state):
            state = list(state)
            for i in range(SCAN):
                n = SCAN * m + i
                base = n * ROWS
                keep = which_ref[n]
                for x, (c, h) in enumerate(pairs):
                    s_ref[c, n, part(h), :] = state[x]
                local = [None] * len(pairs)
                for j in range(ROWS):
                    rows = {
                        c: bcast(um_ref[c, pl.ds(base + j, 1), :])
                        for c in range(t * per, (t + 1) * per)
                    }
                    for x, (c, h) in enumerate(pairs):
                        if j == 0:
                            local[x] = rows[c]
                        else:
                            local[x] = dtab[1, part(h), lane(c)] * local[x] + rows[c]
                for x, (c, h) in enumerate(pairs):
                    state[x] = etab[keep, part(h), lane(c)] * state[x] + local[x]
            return tuple(state)

        zero = jnp.zeros((ROWS, LANES), F32)
        state = lax.fori_loop(0, chunks // SCAN, body, tuple(zero for _ in pairs))
        for x, (c, h) in enumerate(pairs):
            s_ref[c, chunks, part(h), :] = state[x]
            tbuf[count, part(h), lane(c)] = state[x] * ftab[2, part(h), lane(c)]

            @pl.when(me == 0)
            def _():
                passed[part(h), lane(c)] = state[x]

    for r in range(count):
        end = jnp.clip(final[r], 0, tok - 1)
        n = lax.shift_right_logical(end, 3)
        stop = end - n * ROWS
        b = begin[r] - n * ROWS
        where_ref[r] = n
        for j in range(ROWS):
            kind = jnp.where(j > stop, 2, jnp.where(j <= b, 0, 1))
            kind_ref[r, j] = jnp.where(ends_here[r], kind, 0)
            inside = ends_here[r] & (j >= b) & (j <= stop)
            inside_ref[r, j] = jnp.where(inside, 1.0, 0.0).astype(F32)

    def tails(t):
        for r in range(count):
            n = where_ref[r]
            kinds = [kind_ref[r, j] for j in range(ROWS)]
            weights = [inside_ref[r, j] for j in range(ROWS)]
            for c in range(t * per, (t + 1) * per):
                value = [s_ref[c, n, part(h), :] for h in range(halves)]
                for j in range(ROWS):
                    row = bcast(u_ref[c, pl.ds(n * ROWS + j, 1), :]) * weights[j]
                    value = [
                        dtab[kinds[j], part(h), lane(c)] * x + row for h, x in enumerate(value)
                    ]
                for h in range(halves):
                    tbuf[r, part(h), lane(c)] = value[h]

    def span(t):
        return pl.ds(t * width, width)

    def pass_on(t):
        return pltpu.make_async_remote_copy(
            src_ref=passed.at[:, span(t)], dst_ref=arrived.at[:, span(t)],
            send_sem=st_send.at[t], recv_sem=st_recv.at[t],
            device_id={"ctx": me + 1}, device_id_type=MESH,
        )

    def arrival(t):
        return pltpu.make_async_remote_copy(
            src_ref=passed.at[:, span(t)], dst_ref=arrived.at[:, span(t)],
            send_sem=st_send.at[t], recv_sem=st_recv.at[t],
            device_id={"ctx": me - 1}, device_id_type=MESH,
        )

    def relay(t):
        arrival(t).wait_recv()

        @pl.when(me < last)
        def _():
            for c in range(t * per, (t + 1) * per):
                for h in range(halves):
                    passed[part(h), lane(c)] = (
                        s_ref[c, chunks, part(h), :]
                        + ftab[covers, part(h), lane(c)] * arrived[part(h), lane(c)]
                    )
            pass_on(t).start()

    def to_right(i, t):
        return pltpu.make_async_remote_copy(
            src_ref=put_r.at[i, :, span(t)], dst_ref=arr_r.at[i, :, span(t)],
            send_sem=r_send.at[i, t], recv_sem=r_recv.at[i, t],
            device_id={"ctx": me + 1}, device_id_type=MESH,
        )

    def to_left(i, t):
        return pltpu.make_async_remote_copy(
            src_ref=put_l.at[i, :, span(t)], dst_ref=arr_l.at[i, :, span(t)],
            send_sem=l_send.at[i, t], recv_sem=l_recv.at[i, t],
            device_id={"ctx": me - 1}, device_id_type=MESH,
        )

    back = last - me

    def hop(i, t):
        at = span(t)

        @pl.when((me <= i) & (me < last))
        def _():
            own = tbuf[source_of(me + last - i), :, at]
            put_r[i, :, at] = own
            if i:

                @pl.when(me > 0)
                def _():
                    to_right(i - 1, t).wait_recv()
                    put_r[i, :, at] = own + arr_r[i - 1, :, at]

            to_right(i, t).start()

        @pl.when((back <= i) & (back < last))
        def _():
            own = tbuf[source_of(i - back), :, at]
            put_l[i, :, at] = own
            if i:

                @pl.when(back > 0)
                def _():
                    to_left(i - 1, t).wait_recv()
                    put_l[i, :, at] = own + arr_l[i - 1, :, at]

            to_left(i, t).start()

    hops = last
    points = 2 * tiles
    lag = 2

    def serve(point):
        for t in range(tiles):
            if point < points:
                due = (me > 0) & (t + lag * me == point)
            elif t == point - points:
                due = (me > 0) & (t + lag * me >= points)
            else:
                continue

            @pl.when(due)
            def _():
                relay(t)

    def taps(c):
        at = lane(c)
        steps = (iota + 1).astype(F32)
        total = jnp.zeros((ROWS, LANES), F32)
        head = bcast(gain_ref[0:1, at])
        for p in range(poles):
            scale = bcast(cs_ref[pl.ds(p, 1), at])
            value = scale * jnp.exp(bcast(rate_ref[pl.ds(p, 1), at]) * -steps)
            w_ref[c, p] = value
            total = total + value
            head = head + scale
        lead = jnp.where(iota == 0, head, pltpu.roll(total, 1, 0))
        taps = [lead] + [
            jnp.where(iota >= j, pltpu.roll(lead, j, 0), 0.0) for j in range(1, ROWS)
        ]
        for x, a in enumerate(starts):
            base = lax.shift_right_logical(jnp.clip(a, 0, tok - 1), 3) * ROWS
            value = jnp.zeros((ROWS, LANES), F32)
            for j in range(ROWS - 1):
                cut = jnp.int32(ROWS)
                for other in starts:
                    rel = other - base
                    cut = jnp.minimum(cut, jnp.where(rel > j, rel, ROWS))
                row = bcast(u_ref[c, pl.ds(base + j, 1), :])
                value = value - jnp.where(iota >= cut, taps[j], 0.0) * row
            fix_ref[x] = value

        def body(m, _):
            for i in range(FIR):
                n = m * FIR + i
                acc = [fix_ref[which_ref[n]], None]
                for j in range(ROWS):
                    term = taps[j] * bcast(u_ref[c, pl.ds(n * ROWS + j, 1), :])
                    acc[j % 2] = term if acc[j % 2] is None else acc[j % 2] + term
                um_ref[c, pl.ds(pl.multiple_of(n * ROWS, ROWS), ROWS), :] = acc[0] + acc[1]
            return 0

        lax.fori_loop(0, chunks // FIR, body, 0)

    def carry(t):
        pairs = [(c, h) for c in range(t * per, (t + 1) * per) for h in range(halves)]

        def body(m, state):
            state = list(state)
            for i in range(CARRY):
                n = m * CARRY + i
                keep = which_ref[n]
                for x, (c, h) in enumerate(pairs):
                    s_ref[c, n, part(h), :] = s_ref[c, n, part(h), :] + state[x]
                    state[x] = etab[keep, part(h), lane(c)] * state[x]
            return tuple(state)

        lax.fori_loop(
            0, chunks // CARRY, body, tuple(arrived[part(h), lane(c)] for c, h in pairs)
        )

    def emit(c):
        at = lane(c)
        weight = [w_ref[c, p] for p in range(poles)]

        def body(m, _):
            for half in range(EMIT // 2):
                first_row = (EMIT * m + 2 * half) * ROWS
                rows = pl.ds(pl.multiple_of(first_row, 2 * ROWS), 2 * ROWS)
                near = um_ref[c, rows, :]
                made = []
                for i in range(2):
                    n = EMIT * m + 2 * half + i
                    acc = [None] * 4
                    for p in range(poles):
                        term = weight[p] * bcast(s_ref[c, n, pl.ds(p, 1), :])
                        acc[p % 4] = term if acc[p % 4] is None else acc[p % 4] + term
                    total = (acc[0] + acc[1]) + (acc[2] + acc[3])
                    made.append(near[i * ROWS : (i + 1) * ROWS] + mtab[which_ref[n]] * total)
                y = jnp.concatenate(made, axis=0)
                out_ref[rows, at] = (q_ref[rows, at].astype(F32) * y).astype(out_ref.dtype)
            return 0

        lax.fori_loop(0, chunks // EMIT, body, 0)

    for t in range(tiles):
        for copy in loads[t]:
            copy.wait()
        mix(t)
        scan(t)
        if t == 0:
            near = (me > 0).astype(jnp.int32) + (me < last).astype(jnp.int32)
            pl.semaphore_wait(barrier, near)

        @pl.when((me == 0) & (me < last))
        def _():
            pass_on(t).start()

        tails(t)
        hop(0, t)
        serve(t)

    params[1].wait()
    params[2].wait()
    cs_ref[...] = res_ref[...] * jnp.sqrt(1.0 - jnp.exp(-2.0 * rate_ref[...]))
    for t in range(tiles):

        def one(c, _):
            taps(c)
            return 0

        lax.fori_loop(t * per, (t + 1) * per, one, 0)
        if hops > 1:
            hop(1, t)
        serve(tiles + t)

    q_load.wait()
    todo = [(i, t) for i in range(2, hops) for t in range(tiles)]
    for t in range(tiles):
        serve(points + t)

        @pl.when(me > 0)
        def _():
            carry(t)

        for g in range(0, per, 2):
            size = min(2, per - g)

            def one(c, _):
                emit(c)
                return 0

            lax.fori_loop(t * per + g, t * per + g + size, one, 0)
            if t * per + g >= cols // 4 and todo:
                hop(*todo.pop(0))
    for item in todo:
        hop(*item)

    dec_ref[0] = tbuf[source_of(me), :, :]
    for t in range(tiles):
        at = span(t)

        @pl.when(me > 0)
        def _():
            to_right(hops - 1, t).wait_recv()
            dec_ref[0, :, at] = dec_ref[0, :, at] + arr_r[hops - 1, :, at]

        @pl.when(me < last)
        def _():
            to_left(hops - 1, t).wait_recv()
            dec_ref[0, :, at] = dec_ref[0, :, at] + arr_l[hops - 1, :, at]

    for t in range(tiles):

        @pl.when(me < last)
        def _():
            pass_on(t).wait_send()

        for i in range(hops):

            @pl.when((me <= i) & (me < last))
            def _():
                to_right(i, t).wait_send()

            @pl.when((back <= i) & (back < last))
            def _():
                to_left(i, t).wait_send()


def shards(q_feat, k_feat, v_feat, pole_rate, residue, skip_gain, lengths, owners):
    tok, channels = q_feat.shape
    poles, count = pole_rate.shape[0], lengths.shape[0]
    slots = lax.axis_size("ctx")
    cols = channels // LANES
    per = min(4, cols)
    tiles = cols // per
    chunks = tok // ROWS
    hops = max(slots - 1, 1)
    dma = pltpu.SemaphoreType.DMA
    vmem, hbm = pl.BlockSpec(memory_space=pltpu.VMEM), pl.BlockSpec(memory_space=pltpu.HBM)
    state = pltpu.VMEM((poles, channels), F32)
    small = pltpu.VMEM((count, ROWS, LANES), F32)
    block = pltpu.VMEM((hops, poles, channels), F32)
    feat = pltpu.VMEM((tok, channels), q_feat.dtype)
    wide = pltpu.VMEM((cols, tok, LANES), F32)
    args = [
        pltpu.with_memory_space_constraint(x, pltpu.HBM)
        for x in (
            lengths, owners, pole_rate, residue, skip_gain[None, :], k_feat, v_feat, q_feat
        )
    ]
    return pl.pallas_call(
        functools.partial(kernel, tok=tok, poles=poles, count=count, cols=cols, per=per),
        in_specs=[hbm] * 8,
        out_specs=[vmem, vmem],
        out_shape=[
            jax.ShapeDtypeStruct((tok, channels), q_feat.dtype),
            jax.ShapeDtypeStruct((1, poles, channels), F32),
        ],
        scratch_shapes=[
            pltpu.SMEM((count,), jnp.int32), pltpu.SMEM((count,), jnp.int32),
            feat, feat, feat, state, state, pltpu.VMEM((1, channels), F32), wide, wide,
            pltpu.VMEM((cols, chunks + 1, poles, LANES), F32),
            pltpu.VMEM((cols, poles, ROWS, LANES), F32),
            pltpu.VMEM((3, poles, channels), F32),
            pltpu.VMEM((count, poles, channels), F32),
            pltpu.VMEM((3, poles, channels), F32),
            state,
            small, small, small,
            pltpu.VMEM((count + 2, poles, channels), F32),
            state, state, block, block, block, block,
            pltpu.SMEM((chunks,), jnp.int32), pltpu.SMEM((count,), jnp.int32), pltpu.SMEM((count, ROWS), jnp.int32),
            pltpu.SMEM((count, ROWS), F32),
            dma((5,)), dma((tiles, 2)), dma, dma((tiles,)), dma((tiles,)),
            dma((hops, tiles)), dma((hops, tiles)), dma((hops, tiles)), dma((hops, tiles)),
        ],
        compiler_params=pltpu.CompilerParams(
            collective_id=0, has_side_effects=True, vmem_limit_bytes=40 << 20
        ),
        name="modal",
    )(*args)


def solution(mesh):
    tokens = P(("groups", "ctx"), "chan")
    return jax.shard_map(
        shards,
        mesh=mesh,
        in_specs=(
            tokens, tokens, tokens, P(None, "chan"), P(None, "chan"), P("chan"),
            P("groups"), P("groups"),
        ),
        out_specs=(tokens, P(("groups", "ctx"), None, "chan")),
        check_vma=False,
    )
```

```python
import functools

import jax
import jax.numpy as jnp
from jax import lax
from jax.experimental import pallas as pl
from jax.experimental.pallas import tpu as pltpu
from jax.sharding import PartitionSpec as P

F32 = jnp.float32
LANES = 128
ROWS = 8
MIX, SCAN, FIR, CARRY, EMIT = 8, 8, 16, 8, 16
START, SCAN_US, TAPS_US, CARRY_US, EMIT_US = 1.2, 0.43, 0.23, 0.06, 0.36
LINK_US, WIRE_US, QUEUE_US = 0.0105, 2.0, 0.1
MESH = pl.DeviceIdType.MESH


def lane(c):
    if isinstance(c, int):
        return pl.ds(c * LANES, LANES)
    return pl.ds(pl.multiple_of(c * LANES, LANES), LANES)


def kernel(
    lens_hbm, own_hbm, rate_hbm, res_hbm, gain_hbm, k_hbm, v_hbm, q_hbm,
    out_ref, dec_ref,
    lens_ref, own_ref, k_ref, v_ref, q_ref, rate_ref, res_ref, gain_ref, u_ref, um_ref, s_ref, w_ref,
    dtab, etab, ftab, cs_ref, mtab, ltab, fix_ref, tbuf,
    arrived, passed, arr_r, put_r, arr_l, put_l,
    which_ref, where_ref, kind_ref, inside_ref, par_sem, kv_sem, q_sem, st_send, st_recv, r_send, r_recv, l_send, l_recv,
    *, tok, poles, count, cols, per,
):
    slots = lax.axis_size("ctx")
    last = slots - 1
    me = lax.axis_index("ctx")
    tiles = cols // per
    halves = poles // ROWS
    chunks = tok // ROWS
    width = per * LANES
    barrier = pltpu.get_barrier_semaphore()

    for j in range(1, slots):
        pl.semaphore_signal(
            barrier, inc=1, device_id={"ctx": lax.rem(me + j, slots)}, device_id_type=MESH
        )

    params = [
        pltpu.make_async_copy(src, dst, par_sem.at[i])
        for i, (src, dst) in enumerate(
            [
                (rate_hbm, rate_ref), (res_hbm, res_ref), (gain_hbm, gain_ref),
                (lens_hbm, lens_ref), (own_hbm, own_ref),
            ]
        )
    ]
    for i in (3, 4, 0):
        params[i].start()
    loads = []
    for t in range(tiles):
        at = pl.ds(t * width, width)
        loads.append(
            [
                pltpu.make_async_copy(src.at[:, at], dst.at[:, at], kv_sem.at[t, i])
                for i, (src, dst) in enumerate([(k_hbm, k_ref), (v_hbm, v_ref)])
            ]
        )
        for copy in loads[t]:
            copy.start()
    params[1].start()
    params[2].start()
    q_load = pltpu.make_async_copy(q_hbm, q_ref, q_sem)
    q_load.start()

    params[3].wait()
    params[4].wait()
    first = me * tok
    offset = jnp.int32(0)
    begin, final = [], []
    for r in range(count):
        begin.append(offset - first)
        offset = offset + lens_ref[r]
        final.append(offset - 1 - first)
    starts = begin[1:]
    inner = len(starts)
    zero_row = count + 1

    where_in = [lax.shift_right_arithmetic(a, 3) for a in starts]
    rel_in = [lax.bitwise_and(a, ROWS - 1) for a in starts]

    def mark(m, _):
        for i in range(4):
            n = m * 4 + i
            which = jnp.int32(inner)
            for x, chunk in enumerate(where_in):
                which = jnp.where(chunk == n, x, which)
            which_ref[n] = which
        return 0

    lax.fori_loop(0, chunks // 4, mark, 0)

    covers = jnp.int32(1)
    ends_here, goes_on = [], []
    dist = jnp.int32(0)
    for a in starts:
        covers = jnp.where((a >= 0) & (a < tok), 0, covers)
    for r in range(count):
        ends_here.append((final[r] >= 0) & (final[r] < tok))
        goes_on.append((begin[r] < tok) & (final[r] >= tok))
        dist = jnp.where(goes_on[r], final[r] - (tok - 1), dist)

    def source_of(slot):
        row = jnp.int32(zero_row)
        for r in range(count):
            kind = jnp.where(ends_here[r], r, jnp.where(goes_on[r], count, zero_row))
            row = jnp.where(own_ref[r] == slot, kind, row)
        return row

    iota = lax.broadcasted_iota(jnp.int32, (ROWS, LANES), 0)

    def bcast(row):
        return jnp.broadcast_to(row, (ROWS, LANES))

    mtab[inner] = jnp.ones((ROWS, LANES), F32)
    ltab[inner] = jnp.ones((ROWS, LANES), F32)
    for x, chunk in enumerate(where_in):
        low, high = jnp.int32(ROWS), jnp.int32(-1)
        for other, rel in zip(where_in, rel_in):
            low = jnp.where(other == chunk, jnp.minimum(low, rel), low)
            high = jnp.where(other == chunk, jnp.maximum(high, rel), high)
        mtab[x] = jnp.where(iota < low, 1.0, 0.0)
        ltab[x] = jnp.where(iota >= high, 1.0, 0.0)
    fix_ref[inner] = jnp.zeros((ROWS, LANES), F32)
    tbuf[zero_row] = jnp.zeros(tbuf.shape[1:], F32)
    dtab[0] = jnp.zeros(dtab.shape[1:], F32)
    dtab[2] = jnp.ones(dtab.shape[1:], F32)
    for x in range(inner):
        etab[x] = jnp.zeros(etab.shape[1:], F32)
    ftab[0] = jnp.zeros(ftab.shape[1:], F32)
    params[0].wait()
    rate = rate_ref[...]
    dtab[1] = jnp.exp(-rate)
    etab[inner] = jnp.exp(rate * -float(ROWS))
    ftab[1] = jnp.exp(rate * -float(tok))
    ftab[2] = jnp.exp(rate * -dist.astype(F32))

    def part(h):
        return pl.ds(h * ROWS, ROWS)

    def mix(t):
        def body(m, _):
            for half in range(MIX // 2):
                n = MIX * m + 2 * half
                rows = pl.ds(pl.multiple_of(n * ROWS, 2 * ROWS), 2 * ROWS)
                masks = [ltab[which_ref[n + i]] for i in range(2)]
                for c in range(t * per, (t + 1) * per):
                    u = k_ref[rows, lane(c)].astype(F32) * v_ref[rows, lane(c)].astype(F32)
                    u_ref[c, rows, :] = u
                    for i in range(2):
                        at = pl.ds(pl.multiple_of((n + i) * ROWS, ROWS), ROWS)
                        um_ref[c, at, :] = u[i * ROWS : (i + 1) * ROWS] * masks[i]
            return 0

        lax.fori_loop(0, chunks // MIX, body, 0)

    def scan(t):
        pairs = [(c, h) for c in range(t * per, (t + 1) * per) for h in range(halves)]

        def body(m, state):
            state = list(state)
            for i in range(SCAN):
                n = SCAN * m + i
                base = n * ROWS
                keep = which_ref[n]
                for x, (c, h) in enumerate(pairs):
                    s_ref[c, n, part(h), :] = state[x]
                local = [None] * len(pairs)
                for j in range(ROWS):
                    rows = {
                        c: bcast(um_ref[c, pl.ds(base + j, 1), :])
                        for c in range(t * per, (t + 1) * per)
                    }
                    for x, (c, h) in enumerate(pairs):
                        if j == 0:
                            local[x] = rows[c]
                        else:
                            local[x] = dtab[1, part(h), lane(c)] * local[x] + rows[c]
                for x, (c, h) in enumerate(pairs):
                    state[x] = etab[keep, part(h), lane(c)] * state[x] + local[x]
            return tuple(state)

        zero = jnp.zeros((ROWS, LANES), F32)
        steps = chunks // SCAN
        state = lax.fori_loop(0, steps // 2, body, tuple(zero for _ in pairs))
        serve("half", t)
        state = lax.fori_loop(steps // 2, steps, body, state)
        for x, (c, h) in enumerate(pairs):
            s_ref[c, chunks, part(h), :] = state[x]
            tbuf[count, part(h), lane(c)] = state[x] * ftab[2, part(h), lane(c)]

            @pl.when(me == 0)
            def _():
                passed[part(h), lane(c)] = state[x]

    for r in range(count):
        end = jnp.clip(final[r], 0, tok - 1)
        n = lax.shift_right_logical(end, 3)
        stop = end - n * ROWS
        b = begin[r] - n * ROWS
        where_ref[r] = n
        for j in range(ROWS):
            kind = jnp.where(j > stop, 2, jnp.where(j <= b, 0, 1))
            kind_ref[r, j] = jnp.where(ends_here[r], kind, 0)
            inside = ends_here[r] & (j >= b) & (j <= stop)
            inside_ref[r, j] = jnp.where(inside, 1.0, 0.0).astype(F32)

    def tails(t):
        for r in range(count):
            n = where_ref[r]
            kinds = [kind_ref[r, j] for j in range(ROWS)]
            weights = [inside_ref[r, j] for j in range(ROWS)]
            for c in range(t * per, (t + 1) * per):
                value = [s_ref[c, n, part(h), :] for h in range(halves)]
                for j in range(ROWS):
                    row = bcast(u_ref[c, pl.ds(n * ROWS + j, 1), :]) * weights[j]
                    value = [
                        dtab[kinds[j], part(h), lane(c)] * x + row for h, x in enumerate(value)
                    ]
                for h in range(halves):
                    tbuf[r, part(h), lane(c)] = value[h]

    def span(t):
        return pl.ds(t * width, width)

    def pass_on(t):
        return pltpu.make_async_remote_copy(
            src_ref=passed.at[:, span(t)], dst_ref=arrived.at[:, span(t)],
            send_sem=st_send.at[t], recv_sem=st_recv.at[t],
            device_id={"ctx": me + 1}, device_id_type=MESH,
        )

    def arrival(t):
        return pltpu.make_async_remote_copy(
            src_ref=passed.at[:, span(t)], dst_ref=arrived.at[:, span(t)],
            send_sem=st_send.at[t], recv_sem=st_recv.at[t],
            device_id={"ctx": me - 1}, device_id_type=MESH,
        )

    def relay(t):
        arrival(t).wait_recv()

        @pl.when(me < last)
        def _():
            for c in range(t * per, (t + 1) * per):
                for h in range(halves):
                    passed[part(h), lane(c)] = (
                        s_ref[c, chunks, part(h), :]
                        + ftab[covers, part(h), lane(c)] * arrived[part(h), lane(c)]
                    )
            pass_on(t).start()

    def to_right(i, t):
        return pltpu.make_async_remote_copy(
            src_ref=put_r.at[i, :, span(t)], dst_ref=arr_r.at[i, :, span(t)],
            send_sem=r_send.at[i, t], recv_sem=r_recv.at[i, t],
            device_id={"ctx": me + 1}, device_id_type=MESH,
        )

    def to_left(gap, t):
        return pltpu.make_async_remote_copy(
            src_ref=put_l.at[gap - 1, :, span(t)], dst_ref=arr_l.at[gap - 1, :, span(t)],
            send_sem=l_send.at[gap - 1, t], recv_sem=l_recv.at[gap - 1, t],
            device_id={"ctx": me - gap}, device_id_type=MESH,
        )

    def give_left(t):
        for gap in range(last, 0, -1):

            @pl.when(me >= gap)
            def _():
                put_l[gap - 1, :, span(t)] = tbuf[source_of(me - gap), :, span(t)]
                to_left(gap, t).start()

    def hop(m, i, t):
        at = span(t)

        @pl.when(me == m)
        def _():
            own = tbuf[source_of(m + last - i), :, at]
            if m:
                to_right(i - 1, t).wait_recv()
                own = own + arr_r[i - 1, :, at]
            put_r[i, :, at] = own
            to_right(i, t).start()

    hops = last
    group = 2 if per % 2 == 0 else 1
    names, clock, now = [], {}, START
    for t in range(tiles):
        for name in (("half", t), ("scan", t)):
            now += SCAN_US * per / 2
            names.append(name)
            clock[name] = now
    for g in range(cols // group):
        now += TAPS_US * group
        names.append(("taps", g))
        clock[names[-1]] = now
    for g in range(cols // group):
        if g * group % per == 0:
            names.append(("carry", g * group // per))
            clock[names[-1]] = now
            now += CARRY_US * per
        now += EMIT_US * group
        names.append(("emit", g))
        clock[names[-1]] = now
    jobs = {name: [] for name in names}
    send_us = LINK_US * per * poles
    free, reach, open_jobs = [0.0] * slots, {}, []
    for t in range(tiles):
        open_jobs += [("relay", m, 0, t) for m in range(1, slots)]
        open_jobs += [("hop", m, i, t) for i in range(hops) for m in range(i + 1)]
    open_jobs.sort(key=lambda job: (job[0] == "hop", job[2], job[3]))

    def ship(m, now):
        free[m] = max(free[m], now) + send_us
        return free[m] + WIRE_US

    scanned = set()
    for name in names:
        now = clock[name]
        later = min([clock[x] for x in names if clock[x] > now] or [now]) + QUEUE_US
        if name[0] == "scan":
            scanned.add(name[1])
            reach["relay", 1, 0, name[1]] = ship(0, now)
        for job in list(open_jobs):
            kind, m, i, t = job
            if t not in scanned:
                continue
            if kind == "relay":
                ready = reach.get(job, 1e9) <= now and m < last
                ready = ready or name == ("carry", t)
            else:
                ready = (m == 0 or reach.get(("hop", m, i, t), 1e9) <= now)
                ready = ready and free[m] <= later
            if ready:
                jobs[name].append(job)
                open_jobs.remove(job)
                if m < last:
                    after = (kind, m + 1, i + 1 if kind == "hop" else 0, t)
                    reach[after] = ship(m, now)
    open_jobs.sort(key=lambda job: job[2])

    def run(job):
        kind, m, i, t = job
        if kind == "hop":
            hop(m, i, t)
        else:

            @pl.when(me == m)
            def _():
                relay(t)

    def serve(*name):
        for job in jobs[name]:
            run(job)

    def taps(c):
        at = lane(c)
        steps = (iota + 1).astype(F32)
        total = jnp.zeros((ROWS, LANES), F32)
        head = bcast(gain_ref[0:1, at])
        for p in range(poles):
            scale = bcast(cs_ref[pl.ds(p, 1), at])
            value = scale * jnp.exp(bcast(rate_ref[pl.ds(p, 1), at]) * -steps)
            w_ref[c, p] = value
            total = total + value
            head = head + scale
        lead = jnp.where(iota == 0, head, pltpu.roll(total, 1, 0))
        taps = [lead] + [
            jnp.where(iota >= j, pltpu.roll(lead, j, 0), 0.0) for j in range(1, ROWS)
        ]
        for x, a in enumerate(starts):
            base = lax.shift_right_logical(jnp.clip(a, 0, tok - 1), 3) * ROWS
            value = jnp.zeros((ROWS, LANES), F32)
            for j in range(ROWS - 1):
                cut = jnp.int32(ROWS)
                for other in starts:
                    rel = other - base
                    cut = jnp.minimum(cut, jnp.where(rel > j, rel, ROWS))
                row = bcast(u_ref[c, pl.ds(base + j, 1), :])
                value = value - jnp.where(iota >= cut, taps[j], 0.0) * row
            fix_ref[x] = value

        def body(m, _):
            for i in range(FIR):
                n = m * FIR + i
                acc = [fix_ref[which_ref[n]], None]
                for j in range(ROWS):
                    term = taps[j] * bcast(u_ref[c, pl.ds(n * ROWS + j, 1), :])
                    acc[j % 2] = term if acc[j % 2] is None else acc[j % 2] + term
                um_ref[c, pl.ds(pl.multiple_of(n * ROWS, ROWS), ROWS), :] = acc[0] + acc[1]
            return 0

        lax.fori_loop(0, chunks // FIR, body, 0)

    def carry(t):
        pairs = [(c, h) for c in range(t * per, (t + 1) * per) for h in range(halves)]

        def body(m, state):
            state = list(state)
            for i in range(CARRY):
                n = m * CARRY + i
                keep = which_ref[n]
                for x, (c, h) in enumerate(pairs):
                    s_ref[c, n, part(h), :] = s_ref[c, n, part(h), :] + state[x]
                    state[x] = etab[keep, part(h), lane(c)] * state[x]
            return tuple(state)

        lax.fori_loop(
            0, chunks // CARRY, body, tuple(arrived[part(h), lane(c)] for c, h in pairs)
        )

    def emit(c):
        at = lane(c)
        weight = [w_ref[c, p] for p in range(poles)]

        def body(m, _):
            for half in range(EMIT // 2):
                first_row = (EMIT * m + 2 * half) * ROWS
                rows = pl.ds(pl.multiple_of(first_row, 2 * ROWS), 2 * ROWS)
                near = um_ref[c, rows, :]
                made = []
                for i in range(2):
                    n = EMIT * m + 2 * half + i
                    acc = [None] * 4
                    for p in range(poles):
                        term = weight[p] * bcast(s_ref[c, n, pl.ds(p, 1), :])
                        acc[p % 4] = term if acc[p % 4] is None else acc[p % 4] + term
                    total = (acc[0] + acc[1]) + (acc[2] + acc[3])
                    made.append(near[i * ROWS : (i + 1) * ROWS] + mtab[which_ref[n]] * total)
                y = jnp.concatenate(made, axis=0)
                out_ref[rows, at] = (q_ref[rows, at].astype(F32) * y).astype(out_ref.dtype)
            return 0

        lax.fori_loop(0, chunks // EMIT, body, 0)

    for t in range(tiles):
        for copy in loads[t]:
            copy.wait()
        mix(t)
        scan(t)
        if t == 0:
            pl.semaphore_wait(barrier, last)

        @pl.when((me == 0) & (me < last))
        def _():
            pass_on(t).start()

        tails(t)
        give_left(t)
        serve("scan", t)

    params[1].wait()
    params[2].wait()
    cs_ref[...] = res_ref[...] * jnp.sqrt(1.0 - jnp.exp(-2.0 * rate_ref[...]))

    def each(step, g):
        def one(c, _):
            step(c)
            return 0

        lax.fori_loop(g * group, (g + 1) * group, one, 0)

    for g in range(cols // group):
        each(taps, g)
        serve("taps", g)
    q_load.wait()
    for g in range(cols // group):
        if g * group % per == 0:
            t = g * group // per
            serve("carry", t)

            @pl.when(me > 0)
            def _():
                carry(t)

        each(emit, g)
        serve("emit", g)

    for job in open_jobs:
        run(job)

    dec_ref[0] = tbuf[source_of(me), :, :]
    for t in range(tiles):
        at = span(t)

        @pl.when(me > 0)
        def _():
            to_right(hops - 1, t).wait_recv()
            dec_ref[0, :, at] = dec_ref[0, :, at] + arr_r[hops - 1, :, at]

        for gap in range(1, slots):

            @pl.when(me + gap <= last)
            def _():
                to_left(gap, t).wait_recv()
                dec_ref[0, :, at] = dec_ref[0, :, at] + arr_l[gap - 1, :, at]

    for t in range(tiles):

        @pl.when(me < last)
        def _():
            pass_on(t).wait_send()

        for i in range(hops):

            @pl.when((me <= i) & (me < last))
            def _():
                to_right(i, t).wait_send()

            @pl.when(me > i)
            def _():
                to_left(i + 1, t).wait_send()


def shards(q_feat, k_feat, v_feat, pole_rate, residue, skip_gain, lengths, owners):
    tok, channels = q_feat.shape
    poles, count = pole_rate.shape[0], lengths.shape[0]
    slots = lax.axis_size("ctx")
    cols = channels // LANES
    per = min(4, cols)
    tiles = cols // per
    chunks = tok // ROWS
    hops = max(slots - 1, 1)
    dma = pltpu.SemaphoreType.DMA
    vmem, hbm = pl.BlockSpec(memory_space=pltpu.VMEM), pl.BlockSpec(memory_space=pltpu.HBM)
    state = pltpu.VMEM((poles, channels), F32)
    small = pltpu.VMEM((count, ROWS, LANES), F32)
    block = pltpu.VMEM((hops, poles, channels), F32)
    feat = pltpu.VMEM((tok, channels), q_feat.dtype)
    wide = pltpu.VMEM((cols, tok, LANES), F32)
    args = [
        pltpu.with_memory_space_constraint(x, pltpu.HBM)
        for x in (
            lengths, owners, pole_rate, residue, skip_gain[None, :], k_feat, v_feat, q_feat
        )
    ]
    return pl.pallas_call(
        functools.partial(kernel, tok=tok, poles=poles, count=count, cols=cols, per=per),
        in_specs=[hbm] * 8,
        out_specs=[vmem, vmem],
        out_shape=[
            jax.ShapeDtypeStruct((tok, channels), q_feat.dtype),
            jax.ShapeDtypeStruct((1, poles, channels), F32),
        ],
        scratch_shapes=[
            pltpu.SMEM((count,), jnp.int32), pltpu.SMEM((count,), jnp.int32),
            feat, feat, feat, state, state, pltpu.VMEM((1, channels), F32), wide, wide,
            pltpu.VMEM((cols, chunks + 1, poles, LANES), F32),
            pltpu.VMEM((cols, poles, ROWS, LANES), F32),
            pltpu.VMEM((3, poles, channels), F32),
            pltpu.VMEM((count, poles, channels), F32),
            pltpu.VMEM((3, poles, channels), F32),
            state,
            small, small, small,
            pltpu.VMEM((count + 2, poles, channels), F32),
            state, state, block, block, block, block,
            pltpu.SMEM((chunks,), jnp.int32), pltpu.SMEM((count,), jnp.int32), pltpu.SMEM((count, ROWS), jnp.int32),
            pltpu.SMEM((count, ROWS), F32),
            dma((5,)), dma((tiles, 2)), dma, dma((tiles,)), dma((tiles,)),
            dma((hops, tiles)), dma((hops, tiles)), dma((hops, tiles)), dma((hops, tiles)),
        ],
        compiler_params=pltpu.CompilerParams(
            collective_id=0, has_side_effects=True, vmem_limit_bytes=40 << 20
        ),
        name="modal",
    )(*args)


def solution(mesh):
    tokens = P(("groups", "ctx"), "chan")
    return jax.shard_map(
        shards,
        mesh=mesh,
        in_specs=(
            tokens, tokens, tokens, P(None, "chan"), P(None, "chan"), P("chan"),
            P("groups"), P("groups"),
        ),
        out_specs=(tokens, P(("groups", "ctx"), None, "chan")),
        check_vma=False,
    )
```

```python
import functools

import jax
import jax.numpy as jnp
from jax import lax
from jax.experimental import pallas as pl
from jax.experimental.pallas import tpu as pltpu
from jax.sharding import PartitionSpec as P

F32 = jnp.float32
LANES = 128
ROWS = 8
MIX, SCAN, FIR, CARRY, EMIT = 8, 8, 16, 8, 16
START, SCAN_US, TAPS_US, CARRY_US, EMIT_US = 1.2, 0.43, 0.23, 0.06, 0.36
LINK_US, WIRE_US, QUEUE_US = 0.0105, 2.0, 0.1
MESH = pl.DeviceIdType.MESH


def lane(c):
    if isinstance(c, int):
        return pl.ds(c * LANES, LANES)
    return pl.ds(pl.multiple_of(c * LANES, LANES), LANES)


def produce(mask, w_ref, s_ref, near_ref, q_ref, out_ref, at, poles, chunks):
    weight = [w_ref[p] for p in range(poles)]

    def body(m, _):
        for half in range(EMIT // 2):
            first_row = (EMIT * m + 2 * half) * ROWS
            rows = pl.ds(pl.multiple_of(first_row, 2 * ROWS), 2 * ROWS)
            near = near_ref[rows, :]
            made = []
            for i in range(2):
                n = EMIT * m + 2 * half + i
                acc = [None] * 4
                for p in range(poles):
                    term = weight[p] * jnp.broadcast_to(s_ref[n, pl.ds(p, 1), :], (ROWS, LANES))
                    acc[p % 4] = term if acc[p % 4] is None else acc[p % 4] + term
                total = (acc[0] + acc[1]) + (acc[2] + acc[3])
                made.append(near[i * ROWS : (i + 1) * ROWS] + mask(n) * total)
            y = jnp.concatenate(made, axis=0)
            out_ref[rows, at] = (q_ref[rows, at].astype(F32) * y).astype(out_ref.dtype)
        return 0

    lax.fori_loop(0, chunks // EMIT, body, 0)


def finish(dec_ref, s_ref, near_ref, w_ref, q_ref, mask_ref, *rest, poles, chunks, per, ahead):
    rest = list(rest)
    head_ref = rest.pop(0) if ahead else None
    out_hbm, dec_hbm, made_ref, sem = rest
    copies = [pltpu.make_async_copy(dec_ref, dec_hbm, sem.at[0])]
    edge = ahead * per * LANES
    if ahead:
        copies.append(pltpu.make_async_copy(head_ref, out_hbm.at[:, pl.ds(0, edge)], sem.at[1]))
    for copy in copies:
        copy.start()
    for c in range(per):
        produce(
            lambda n: mask_ref[n], w_ref.at[c], s_ref.at[c], near_ref.at[c],
            q_ref, made_ref, lane(c), poles, chunks,
        )
        copies.append(
            pltpu.make_async_copy(
                made_ref.at[:, lane(c)],
                out_hbm.at[:, pl.ds(edge + c * LANES, LANES)], sem.at[2 + c],
            )
        )
        copies[-1].start()
    for copy in copies:
        copy.wait()


def kernel(
    lens_hbm, own_hbm, rate_hbm, res_hbm, gain_hbm, k_hbm, v_hbm, q_hbm,
    dec_ref, s_out, um_out, w_out, qt_ref, mask_ref, *rest,
    tok, poles, count, cols, per,
):
    tiles = cols // per
    ahead = tiles - 1
    rest = list(rest)
    out_ref, q_ref = (rest.pop(0), rest.pop(0)) if ahead else (None, None)
    s_all = [rest.pop(0) for _ in range(ahead)] + [s_out]
    um_all = [rest.pop(0) for _ in range(ahead)] + [um_out]
    w_all = [rest.pop(0) for _ in range(ahead)] + [w_out]
    (
        lens_ref, own_ref, k_ref, v_ref, rate_ref, res_ref, gain_ref, u_ref,
        dtab, etab, ftab, cs_ref, mtab, ltab, fix_ref, tbuf,
        arrived, passed, arr_r, put_r, arr_l, put_l,
        which_ref, where_ref, kind_ref, inside_ref,
        par_sem, kv_sem, q_sem, st_send, st_recv, r_send, r_recv, l_send, l_recv,
    ) = rest
    slots = lax.axis_size("ctx")
    last = slots - 1
    me = lax.axis_index("ctx")
    halves = poles // ROWS
    chunks = tok // ROWS
    width = per * LANES
    barrier = pltpu.get_barrier_semaphore()

    for j in range(1, slots):
        pl.semaphore_signal(
            barrier, inc=1, device_id={"ctx": lax.rem(me + j, slots)}, device_id_type=MESH
        )

    params = [
        pltpu.make_async_copy(src, dst, par_sem.at[i])
        for i, (src, dst) in enumerate(
            [
                (rate_hbm, rate_ref), (res_hbm, res_ref), (gain_hbm, gain_ref),
                (lens_hbm, lens_ref), (own_hbm, own_ref),
            ]
        )
    ]
    for i in (3, 4, 0):
        params[i].start()
    loads = []
    for t in range(tiles):
        at = pl.ds(t * width, width)
        loads.append(
            [
                pltpu.make_async_copy(src.at[:, at], dst.at[:, at], kv_sem.at[t, i])
                for i, (src, dst) in enumerate([(k_hbm, k_ref), (v_hbm, v_ref)])
            ]
        )
        for copy in loads[t]:
            copy.start()
    params[1].start()
    params[2].start()
    edge = ahead * width
    q_loads = [pltpu.make_async_copy(q_hbm.at[:, pl.ds(edge, width)], qt_ref, q_sem.at[0])]
    if ahead:
        q_loads.append(
            pltpu.make_async_copy(q_hbm.at[:, pl.ds(0, edge)], q_ref, q_sem.at[1])
        )
    for copy in q_loads:
        copy.start()

    params[3].wait()
    params[4].wait()
    first = me * tok
    offset = jnp.int32(0)
    begin, final = [], []
    for r in range(count):
        begin.append(offset - first)
        offset = offset + lens_ref[r]
        final.append(offset - 1 - first)
    starts = begin[1:]
    inner = len(starts)
    zero_row = count + 1

    where_in = [lax.shift_right_arithmetic(a, 3) for a in starts]
    rel_in = [lax.bitwise_and(a, ROWS - 1) for a in starts]

    def mark(m, _):
        for i in range(4):
            n = m * 4 + i
            which = jnp.int32(inner)
            for x, chunk in enumerate(where_in):
                which = jnp.where(chunk == n, x, which)
            which_ref[n] = which
        return 0

    lax.fori_loop(0, chunks // 4, mark, 0)

    covers = jnp.int32(1)
    ends_here, goes_on = [], []
    dist = jnp.int32(0)
    for a in starts:
        covers = jnp.where((a >= 0) & (a < tok), 0, covers)
    for r in range(count):
        ends_here.append((final[r] >= 0) & (final[r] < tok))
        goes_on.append((begin[r] < tok) & (final[r] >= tok))
        dist = jnp.where(goes_on[r], final[r] - (tok - 1), dist)

    def source_of(slot):
        row = jnp.int32(zero_row)
        for r in range(count):
            kind = r if r < count - 1 else count
            kind = jnp.where(ends_here[r], kind, jnp.where(goes_on[r], count, zero_row))
            row = jnp.where(own_ref[r] == slot, kind, row)
        return row

    iota = lax.broadcasted_iota(jnp.int32, (ROWS, LANES), 0)

    def bcast(row):
        return jnp.broadcast_to(row, (ROWS, LANES))

    mtab[inner] = jnp.ones((ROWS, LANES), F32)
    ltab[inner] = jnp.ones((ROWS, LANES), F32)
    for x, chunk in enumerate(where_in):
        low, high = jnp.int32(ROWS), jnp.int32(-1)
        for other, rel in zip(where_in, rel_in):
            low = jnp.where(other == chunk, jnp.minimum(low, rel), low)
            high = jnp.where(other == chunk, jnp.maximum(high, rel), high)
        mtab[x] = jnp.where(iota < low, 1.0, 0.0)
        ltab[x] = jnp.where(iota >= high, 1.0, 0.0)

    def cover(m, _):
        for i in range(8):
            mask_ref[m * 8 + i] = mtab[which_ref[m * 8 + i]]
        return 0

    lax.fori_loop(0, chunks // 8, cover, 0)
    fix_ref[inner] = jnp.zeros((ROWS, LANES), F32)
    tbuf[zero_row] = jnp.zeros(tbuf.shape[1:], F32)
    dtab[0] = jnp.zeros(dtab.shape[1:], F32)
    dtab[2] = jnp.ones(dtab.shape[1:], F32)
    for x in range(inner):
        etab[x] = jnp.zeros(etab.shape[1:], F32)
    ftab[0] = jnp.zeros(ftab.shape[1:], F32)
    params[0].wait()
    rate = rate_ref[...]
    dtab[1] = jnp.exp(-rate)
    etab[inner] = jnp.exp(rate * -float(ROWS))
    ftab[1] = jnp.exp(rate * -float(tok))
    ftab[2] = jnp.exp(rate * -dist.astype(F32))

    def part(h):
        return pl.ds(h * ROWS, ROWS)

    def mix(t):
        def body(m, _):
            for half in range(MIX // 2):
                n = MIX * m + 2 * half
                rows = pl.ds(pl.multiple_of(n * ROWS, 2 * ROWS), 2 * ROWS)
                masks = [ltab[which_ref[n + i]] for i in range(2)]
                for c in range(t * per, (t + 1) * per):
                    u = k_ref[rows, lane(c)].astype(F32) * v_ref[rows, lane(c)].astype(F32)
                    u_ref[c, rows, :] = u
                    for i in range(2):
                        at = pl.ds(pl.multiple_of((n + i) * ROWS, ROWS), ROWS)
                        um_all[t][c - t * per, at, :] = u[i * ROWS : (i + 1) * ROWS] * masks[i]
            return 0

        lax.fori_loop(0, chunks // MIX, body, 0)

    def scan(t):
        pairs = [(c, h) for c in range(t * per, (t + 1) * per) for h in range(halves)]

        def body(m, state):
            state = list(state)
            for i in range(SCAN):
                n = SCAN * m + i
                base = n * ROWS
                keep = which_ref[n]
                for x, (c, h) in enumerate(pairs):
                    s_all[t][c - t * per, n, part(h), :] = state[x]
                local = [None] * len(pairs)
                for j in range(ROWS):
                    rows = {
                        c: bcast(um_all[t][c - t * per, pl.ds(base + j, 1), :])
                        for c in range(t * per, (t + 1) * per)
                    }
                    for x, (c, h) in enumerate(pairs):
                        if j == 0:
                            local[x] = rows[c]
                        else:
                            local[x] = dtab[1, part(h), lane(c)] * local[x] + rows[c]
                for x, (c, h) in enumerate(pairs):
                    state[x] = etab[keep, part(h), lane(c)] * state[x] + local[x]
            return tuple(state)

        zero = jnp.zeros((ROWS, LANES), F32)
        steps = chunks // SCAN
        state = lax.fori_loop(0, steps // 2, body, tuple(zero for _ in pairs))
        serve("half", t)
        state = lax.fori_loop(steps // 2, steps, body, state)
        for x, (c, h) in enumerate(pairs):
            s_all[t][c - t * per, chunks, part(h), :] = state[x]
            tbuf[count, part(h), lane(c)] = state[x] * ftab[2, part(h), lane(c)]

            @pl.when(me == 0)
            def _():
                passed[part(h), lane(c)] = state[x]

    for r in range(count - 1):
        end = jnp.clip(final[r], 0, tok - 1)
        n = lax.shift_right_logical(end, 3)
        stop = end - n * ROWS
        b = begin[r] - n * ROWS
        where_ref[r] = n
        for j in range(ROWS):
            kind = jnp.where(j > stop, 2, jnp.where(j <= b, 0, 1))
            kind_ref[r, j] = jnp.where(ends_here[r], kind, 0)
            inside = ends_here[r] & (j >= b) & (j <= stop)
            inside_ref[r, j] = jnp.where(inside, 1.0, 0.0).astype(F32)

    def tails(t):
        for r in range(count - 1):
            n = where_ref[r]
            kinds = [kind_ref[r, j] for j in range(ROWS)]
            weights = [inside_ref[r, j] for j in range(ROWS)]
            for c in range(t * per, (t + 1) * per):
                value = [s_all[t][c - t * per, n, part(h), :] for h in range(halves)]
                for j in range(ROWS):
                    row = bcast(u_ref[c, pl.ds(n * ROWS + j, 1), :]) * weights[j]
                    value = [
                        dtab[kinds[j], part(h), lane(c)] * x + row for h, x in enumerate(value)
                    ]
                for h in range(halves):
                    tbuf[r, part(h), lane(c)] = value[h]

    def span(t):
        return pl.ds(t * width, width)

    def pass_on(t):
        return pltpu.make_async_remote_copy(
            src_ref=passed.at[:, span(t)], dst_ref=arrived.at[:, span(t)],
            send_sem=st_send.at[t], recv_sem=st_recv.at[t],
            device_id={"ctx": me + 1}, device_id_type=MESH,
        )

    def arrival(t):
        return pltpu.make_async_remote_copy(
            src_ref=passed.at[:, span(t)], dst_ref=arrived.at[:, span(t)],
            send_sem=st_send.at[t], recv_sem=st_recv.at[t],
            device_id={"ctx": me - 1}, device_id_type=MESH,
        )

    def relay(t):
        arrival(t).wait_recv()

        @pl.when(me < last)
        def _():
            for c in range(t * per, (t + 1) * per):
                for h in range(halves):
                    passed[part(h), lane(c)] = (
                        s_all[t][c - t * per, chunks, part(h), :]
                        + ftab[covers, part(h), lane(c)] * arrived[part(h), lane(c)]
                    )
            pass_on(t).start()

    def to_right(i, t):
        return pltpu.make_async_remote_copy(
            src_ref=put_r.at[i, :, span(t)], dst_ref=arr_r.at[i, :, span(t)],
            send_sem=r_send.at[i, t], recv_sem=r_recv.at[i, t],
            device_id={"ctx": me + 1}, device_id_type=MESH,
        )

    def to_left(gap, t):
        return pltpu.make_async_remote_copy(
            src_ref=put_l.at[gap - 1, :, span(t)], dst_ref=arr_l.at[gap - 1, :, span(t)],
            send_sem=l_send.at[gap - 1, t], recv_sem=l_recv.at[gap - 1, t],
            device_id={"ctx": me - gap}, device_id_type=MESH,
        )

    def give_left(t):
        for gap in range(last, 0, -1):

            @pl.when(me >= gap)
            def _():
                put_l[gap - 1, :, span(t)] = tbuf[source_of(me - gap), :, span(t)]
                to_left(gap, t).start()

    def hop(m, i, t):
        at = span(t)

        @pl.when(me == m)
        def _():
            own = tbuf[source_of(m + last - i), :, at]
            if m:
                to_right(i - 1, t).wait_recv()
                own = own + arr_r[i - 1, :, at]
            put_r[i, :, at] = own
            to_right(i, t).start()

    hops = last
    group = 2 if per % 2 == 0 else 1
    names, clock, now = [], {}, START
    for t in range(tiles):
        for name in (("half", t), ("scan", t)):
            now += SCAN_US * per / 2
            names.append(name)
            clock[name] = now
    for g in range(cols // group):
        now += TAPS_US * group
        names.append(("taps", g))
        clock[names[-1]] = now
    for g in range(cols // group):
        if g * group % per == 0:
            names.append(("carry", g * group // per))
            clock[names[-1]] = now
            now += CARRY_US * per
        now += EMIT_US * group if g * group < (tiles - 1) * per else 0.0
        names.append(("emit", g))
        clock[names[-1]] = now
    jobs = {name: [] for name in names}
    send_us = LINK_US * per * poles
    free, reach, open_jobs = [0.0] * slots, {}, []
    for t in range(tiles):
        open_jobs += [("relay", m, 0, t) for m in range(1, slots)]
        open_jobs += [("hop", m, i, t) for i in range(hops) for m in range(i + 1)]
    open_jobs.sort(key=lambda job: (job[0] == "hop", job[2], job[3]))

    def ship(m, now):
        free[m] = max(free[m], now) + send_us
        return free[m] + WIRE_US

    scanned = set()
    for name in names:
        now = clock[name]
        later = min([clock[x] for x in names if clock[x] > now] or [now]) + QUEUE_US
        if name[0] == "scan":
            scanned.add(name[1])
            reach["relay", 1, 0, name[1]] = ship(0, now)
        for job in list(open_jobs):
            kind, m, i, t = job
            if t not in scanned:
                continue
            if kind == "relay":
                ready = reach.get(job, 1e9) <= now and m < last
                ready = ready or name == ("carry", t)
            else:
                ready = (m == 0 or reach.get(("hop", m, i, t), 1e9) <= now)
                ready = ready and free[m] <= later
            if ready:
                jobs[name].append(job)
                open_jobs.remove(job)
                if m < last:
                    after = (kind, m + 1, i + 1 if kind == "hop" else 0, t)
                    reach[after] = ship(m, now)
    open_jobs.sort(key=lambda job: job[2])

    def run(job):
        kind, m, i, t = job
        if kind == "hop":
            hop(m, i, t)
        else:

            @pl.when(me == m)
            def _():
                relay(t)

    def serve(*name):
        for job in jobs[name]:
            run(job)

    def taps(t, c):
        at = lane(c)
        steps = (iota + 1).astype(F32)
        total = jnp.zeros((ROWS, LANES), F32)
        head = bcast(gain_ref[0:1, at])
        for p in range(poles):
            scale = bcast(cs_ref[pl.ds(p, 1), at])
            value = scale * jnp.exp(bcast(rate_ref[pl.ds(p, 1), at]) * -steps)
            w_all[t][c - t * per, p] = value
            total = total + value
            head = head + scale
        lead = jnp.where(iota == 0, head, pltpu.roll(total, 1, 0))
        taps = [lead] + [
            jnp.where(iota >= j, pltpu.roll(lead, j, 0), 0.0) for j in range(1, ROWS)
        ]
        for x, a in enumerate(starts):
            base = lax.shift_right_logical(jnp.clip(a, 0, tok - 1), 3) * ROWS
            value = jnp.zeros((ROWS, LANES), F32)
            for j in range(ROWS - 1):
                cut = jnp.int32(ROWS)
                for other in starts:
                    rel = other - base
                    cut = jnp.minimum(cut, jnp.where(rel > j, rel, ROWS))
                row = bcast(u_ref[c, pl.ds(base + j, 1), :])
                value = value - jnp.where(iota >= cut, taps[j], 0.0) * row
            fix_ref[x] = value

        def body(m, _):
            for i in range(FIR):
                n = m * FIR + i
                acc = [fix_ref[which_ref[n]], None]
                for j in range(ROWS):
                    term = taps[j] * bcast(u_ref[c, pl.ds(n * ROWS + j, 1), :])
                    acc[j % 2] = term if acc[j % 2] is None else acc[j % 2] + term
                um_all[t][c - t * per, pl.ds(pl.multiple_of(n * ROWS, ROWS), ROWS), :] = acc[0] + acc[1]
            return 0

        lax.fori_loop(0, chunks // FIR, body, 0)

    def carry(t):
        pairs = [(c, h) for c in range(t * per, (t + 1) * per) for h in range(halves)]

        def body(m, state):
            state = list(state)
            for i in range(CARRY):
                n = m * CARRY + i
                keep = which_ref[n]
                for x, (c, h) in enumerate(pairs):
                    s_all[t][c - t * per, n, part(h), :] = s_all[t][c - t * per, n, part(h), :] + state[x]
                    state[x] = etab[keep, part(h), lane(c)] * state[x]
            return tuple(state)

        lax.fori_loop(
            0, chunks // CARRY, body, tuple(arrived[part(h), lane(c)] for c, h in pairs)
        )

    def emit(t, c):
        local = c - t * per
        produce(
            lambda n: mtab[which_ref[n]], w_all[t].at[local], s_all[t].at[local],
            um_all[t].at[local], q_ref, out_ref, lane(c), poles, chunks,
        )

    for t in range(tiles):
        for copy in loads[t]:
            copy.wait()
        mix(t)
        scan(t)
        if t == 0:
            pl.semaphore_wait(barrier, last)

        @pl.when((me == 0) & (me < last))
        def _():
            pass_on(t).start()

        tails(t)
        give_left(t)
        serve("scan", t)

    params[1].wait()
    params[2].wait()
    cs_ref[...] = res_ref[...] * jnp.sqrt(1.0 - jnp.exp(-2.0 * rate_ref[...]))

    def each(step, g):
        def one(c, _):
            step(g * group // per, c)
            return 0

        lax.fori_loop(g * group, (g + 1) * group, one, 0)

    for g in range(cols // group):
        each(taps, g)
        serve("taps", g)
    for copy in q_loads:
        copy.wait()
    for g in range(cols // group):
        if g * group % per == 0:
            t = g * group // per
            serve("carry", t)

            @pl.when(me > 0)
            def _():
                carry(t)

        if g * group < ahead * per:
            each(emit, g)
        serve("emit", g)

    for job in open_jobs:
        run(job)

    dec_ref[0] = tbuf[source_of(me), :, :]
    for t in range(tiles):
        at = span(t)

        @pl.when(me > 0)
        def _():
            to_right(hops - 1, t).wait_recv()
            dec_ref[0, :, at] = dec_ref[0, :, at] + arr_r[hops - 1, :, at]

        for gap in range(1, slots):

            @pl.when(me + gap <= last)
            def _():
                to_left(gap, t).wait_recv()
                dec_ref[0, :, at] = dec_ref[0, :, at] + arr_l[gap - 1, :, at]

    for t in range(tiles):

        @pl.when(me < last)
        def _():
            pass_on(t).wait_send()

        for i in range(hops):

            @pl.when((me <= i) & (me < last))
            def _():
                to_right(i, t).wait_send()

            @pl.when(me > i)
            def _():
                to_left(i + 1, t).wait_send()


def shards(q_feat, k_feat, v_feat, pole_rate, residue, skip_gain, lengths, owners):
    tok, channels = q_feat.shape
    poles, count = pole_rate.shape[0], lengths.shape[0]
    slots = lax.axis_size("ctx")
    cols = channels // LANES
    per = min(4, cols)
    tiles = cols // per
    chunks = tok // ROWS
    hops = max(slots - 1, 1)
    dma = pltpu.SemaphoreType.DMA
    vmem, hbm = pl.BlockSpec(memory_space=pltpu.VMEM), pl.BlockSpec(memory_space=pltpu.HBM)
    ahead = tiles - 1
    width = per * LANES
    edge = ahead * width
    state = pltpu.VMEM((poles, channels), F32)
    small = pltpu.VMEM((count, ROWS, LANES), F32)
    block = pltpu.VMEM((hops, poles, channels), F32)
    feat = pltpu.VMEM((tok, channels), q_feat.dtype)
    s_shape, near_shape = (per, chunks + 1, poles, LANES), (per, tok, LANES)
    w_shape = (per, poles, ROWS, LANES)
    handed = [
        jax.ShapeDtypeStruct((1, poles, channels), F32),
        jax.ShapeDtypeStruct(s_shape, F32),
        jax.ShapeDtypeStruct(near_shape, F32),
        jax.ShapeDtypeStruct(w_shape, F32),
        jax.ShapeDtypeStruct((tok, width), q_feat.dtype),
        jax.ShapeDtypeStruct((chunks, ROWS, LANES), F32),
    ]
    early = []
    if ahead:
        handed.append(jax.ShapeDtypeStruct((tok, edge), q_feat.dtype))
        early = [pltpu.VMEM((tok, edge), q_feat.dtype)]
    args = [
        pltpu.with_memory_space_constraint(x, pltpu.HBM)
        for x in (
            lengths, owners, pole_rate, residue, skip_gain[None, :], k_feat, v_feat, q_feat
        )
    ]
    handed = pl.pallas_call(
        functools.partial(kernel, tok=tok, poles=poles, count=count, cols=cols, per=per),
        in_specs=[hbm] * 8,
        out_specs=[vmem] * len(handed),
        out_shape=handed,
        scratch_shapes=early
        + [pltpu.VMEM(s_shape, F32)] * ahead
        + [pltpu.VMEM(near_shape, F32)] * ahead
        + [pltpu.VMEM(w_shape, F32)] * ahead
        + [
            pltpu.SMEM((count,), jnp.int32), pltpu.SMEM((count,), jnp.int32),
            feat, feat, state, state, pltpu.VMEM((1, channels), F32),
            pltpu.VMEM((cols, tok, LANES), F32),
            pltpu.VMEM((3, poles, channels), F32),
            pltpu.VMEM((count, poles, channels), F32),
            pltpu.VMEM((3, poles, channels), F32),
            state,
            small, small, small,
            pltpu.VMEM((count + 2, poles, channels), F32),
            state, state, block, block, block, block,
            pltpu.SMEM((chunks,), jnp.int32), pltpu.SMEM((count,), jnp.int32),
            pltpu.SMEM((count, ROWS), jnp.int32), pltpu.SMEM((count, ROWS), F32),
            dma((5,)), dma((tiles, 2)), dma((2,)), dma((tiles,)), dma((tiles,)),
            dma((hops, tiles)), dma((hops, tiles)), dma((hops, tiles)), dma((hops, tiles)),
        ],
        compiler_params=pltpu.CompilerParams(
            collective_id=0, has_side_effects=True, vmem_limit_bytes=40 << 20
        ),
        name="modal",
    )(*args)
    return pl.pallas_call(
        functools.partial(finish, poles=poles, chunks=chunks, per=per, ahead=ahead),
        in_specs=[vmem] * len(handed),
        out_specs=[hbm, hbm],
        out_shape=[
            jax.ShapeDtypeStruct((tok, channels), q_feat.dtype),
            jax.ShapeDtypeStruct((1, poles, channels), F32),
        ],
        scratch_shapes=[pltpu.VMEM((tok, width), q_feat.dtype), dma((2 + per,))],
        compiler_params=pltpu.CompilerParams(vmem_limit_bytes=8 << 20),
        name="tail",
    )(*handed)


def solution(mesh):
    tokens = P(("groups", "ctx"), "chan")
    return jax.shard_map(
        shards,
        mesh=mesh,
        in_specs=(
            tokens, tokens, tokens, P(None, "chan"), P(None, "chan"), P("chan"),
            P("groups"), P("groups"),
        ),
        out_specs=(tokens, P(("groups", "ctx"), None, "chan")),
        check_vma=False,
    )
```

```python
import functools

import jax
import jax.numpy as jnp
from jax import lax
from jax.experimental import pallas as pl
from jax.experimental.pallas import tpu as pltpu
from jax.sharding import PartitionSpec as P

F32 = jnp.float32
LANES = 128
ROWS = 8
MIX, SCAN, FIR, CARRY, EMIT = 8, 8, 16, 8, 16
START, SCAN_US, TAPS_US, CARRY_US, EMIT_US = 1.2, 0.43, 0.23, 0.06, 0.36
LINK_US, WIRE_US, QUEUE_US = 0.0105, 2.0, 0.1
MESH = pl.DeviceIdType.MESH


def lane(c):
    if isinstance(c, int):
        return pl.ds(c * LANES, LANES)
    return pl.ds(pl.multiple_of(c * LANES, LANES), LANES)


def produce(mask, w_ref, s_ref, near_ref, q_ref, out_ref, at, poles, chunks):
    weight = [w_ref[p] for p in range(poles)]

    def body(m, _):
        for half in range(EMIT // 2):
            first_row = (EMIT * m + 2 * half) * ROWS
            rows = pl.ds(pl.multiple_of(first_row, 2 * ROWS), 2 * ROWS)
            near = near_ref[rows, :]
            made = []
            for i in range(2):
                n = EMIT * m + 2 * half + i
                acc = [None] * 4
                for p in range(poles):
                    term = weight[p] * jnp.broadcast_to(s_ref[n, pl.ds(p, 1), :], (ROWS, LANES))
                    acc[p % 4] = term if acc[p % 4] is None else acc[p % 4] + term
                total = (acc[0] + acc[1]) + (acc[2] + acc[3])
                made.append(near[i * ROWS : (i + 1) * ROWS] + mask(n) * total)
            y = jnp.concatenate(made, axis=0)
            out_ref[rows, at] = (q_ref[rows, at].astype(F32) * y).astype(out_ref.dtype)
        return 0

    lax.fori_loop(0, chunks // EMIT, body, 0)


def finish(dec_ref, s_ref, near_ref, w_ref, q_ref, mask_ref, *rest, poles, chunks, per, late, made):
    rest = list(rest)
    head_ref = rest.pop(0) if made else None
    out_hbm, dec_hbm, made_ref, sem = rest
    copies = [pltpu.make_async_copy(dec_ref, dec_hbm, sem.at[0])]
    edge = made * LANES
    if made:
        copies.append(pltpu.make_async_copy(head_ref, out_hbm.at[:, pl.ds(0, edge)], sem.at[1]))
    for copy in copies:
        copy.start()
    for c in range(late):
        x = per - late + c
        produce(
            lambda n: mask_ref[n], w_ref.at[x], s_ref.at[x], near_ref.at[x],
            q_ref, made_ref, lane(c), poles, chunks,
        )
        copies.append(
            pltpu.make_async_copy(
                made_ref.at[:, lane(c)],
                out_hbm.at[:, pl.ds(edge + c * LANES, LANES)], sem.at[2 + c],
            )
        )
        copies[-1].start()
    for copy in copies:
        copy.wait()


def kernel(
    lens_hbm, own_hbm, rate_hbm, res_hbm, gain_hbm, k_hbm, v_hbm, q_hbm,
    dec_ref, s_out, um_out, w_out, qt_ref, mask_ref, *rest,
    tok, poles, count, cols, per, late,
):
    tiles = cols // per
    ahead = tiles - 1
    rest = list(rest)
    made = cols - late
    out_ref, q_ref = (rest.pop(0), rest.pop(0)) if made else (None, None)
    s_all = [rest.pop(0) for _ in range(ahead)] + [s_out]
    um_all = [rest.pop(0) for _ in range(ahead)] + [um_out]
    w_all = [rest.pop(0) for _ in range(ahead)] + [w_out]
    (
        lens_ref, own_ref, k_ref, v_ref, rate_ref, res_ref, gain_ref, u_ref,
        dtab, etab, ftab, cs_ref, mtab, ltab, fix_ref, tbuf,
        arrived, passed, arr_r, put_r, arr_l, put_l,
        which_ref, where_ref, kind_ref, inside_ref,
        par_sem, kv_sem, q_sem, st_send, st_recv, r_send, r_recv, l_send, l_recv,
    ) = rest
    slots = lax.axis_size("ctx")
    last = slots - 1
    me = lax.axis_index("ctx")
    halves = poles // ROWS
    chunks = tok // ROWS
    width = per * LANES
    barrier = pltpu.get_barrier_semaphore()

    for j in range(1, slots):
        pl.semaphore_signal(
            barrier, inc=1, device_id={"ctx": lax.rem(me + j, slots)}, device_id_type=MESH
        )

    params = [
        pltpu.make_async_copy(src, dst, par_sem.at[i])
        for i, (src, dst) in enumerate(
            [
                (rate_hbm, rate_ref), (res_hbm, res_ref), (gain_hbm, gain_ref),
                (lens_hbm, lens_ref), (own_hbm, own_ref),
            ]
        )
    ]
    for i in (3, 4, 0):
        params[i].start()
    loads = []
    for t in range(tiles):
        at = pl.ds(t * width, width)
        loads.append(
            [
                pltpu.make_async_copy(src.at[:, at], dst.at[:, at], kv_sem.at[t, i])
                for i, (src, dst) in enumerate([(k_hbm, k_ref), (v_hbm, v_ref)])
            ]
        )
        for copy in loads[t]:
            copy.start()
    params[1].start()
    params[2].start()
    edge = made * LANES
    q_loads = [
        pltpu.make_async_copy(q_hbm.at[:, pl.ds(edge, late * LANES)], qt_ref, q_sem.at[0])
    ]
    if made:
        q_loads.append(
            pltpu.make_async_copy(q_hbm.at[:, pl.ds(0, edge)], q_ref, q_sem.at[1])
        )
    for copy in q_loads:
        copy.start()

    params[3].wait()
    params[4].wait()
    first = me * tok
    offset = jnp.int32(0)
    begin, final = [], []
    for r in range(count):
        begin.append(offset - first)
        offset = offset + lens_ref[r]
        final.append(offset - 1 - first)
    starts = begin[1:]
    inner = len(starts)
    zero_row = count + 1

    where_in = [lax.shift_right_arithmetic(a, 3) for a in starts]
    rel_in = [lax.bitwise_and(a, ROWS - 1) for a in starts]

    def mark(m, _):
        for i in range(4):
            n = m * 4 + i
            which = jnp.int32(inner)
            for x, chunk in enumerate(where_in):
                which = jnp.where(chunk == n, x, which)
            which_ref[n] = which
        return 0

    lax.fori_loop(0, chunks // 4, mark, 0)

    covers = jnp.int32(1)
    ends_here, goes_on = [], []
    dist = jnp.int32(0)
    for a in starts:
        covers = jnp.where((a >= 0) & (a < tok), 0, covers)
    for r in range(count):
        ends_here.append((final[r] >= 0) & (final[r] < tok))
        goes_on.append((begin[r] < tok) & (final[r] >= tok))
        dist = jnp.where(goes_on[r], final[r] - (tok - 1), dist)

    def source_of(slot):
        row = jnp.int32(zero_row)
        for r in range(count):
            kind = r if r < count - 1 else count
            kind = jnp.where(ends_here[r], kind, jnp.where(goes_on[r], count, zero_row))
            row = jnp.where(own_ref[r] == slot, kind, row)
        return row

    iota = lax.broadcasted_iota(jnp.int32, (ROWS, LANES), 0)

    def bcast(row):
        return jnp.broadcast_to(row, (ROWS, LANES))

    mtab[inner] = jnp.ones((ROWS, LANES), F32)
    ltab[inner] = jnp.ones((ROWS, LANES), F32)
    for x, chunk in enumerate(where_in):
        low, high = jnp.int32(ROWS), jnp.int32(-1)
        for other, rel in zip(where_in, rel_in):
            low = jnp.where(other == chunk, jnp.minimum(low, rel), low)
            high = jnp.where(other == chunk, jnp.maximum(high, rel), high)
        mtab[x] = jnp.where(iota < low, 1.0, 0.0)
        ltab[x] = jnp.where(iota >= high, 1.0, 0.0)

    def cover(m, _):
        for i in range(8):
            mask_ref[m * 8 + i] = mtab[which_ref[m * 8 + i]]
        return 0

    lax.fori_loop(0, chunks // 8, cover, 0)
    fix_ref[inner] = jnp.zeros((ROWS, LANES), F32)
    tbuf[zero_row] = jnp.zeros(tbuf.shape[1:], F32)
    dtab[0] = jnp.zeros(dtab.shape[1:], F32)
    dtab[2] = jnp.ones(dtab.shape[1:], F32)
    for x in range(inner):
        etab[x] = jnp.zeros(etab.shape[1:], F32)
    ftab[0] = jnp.zeros(ftab.shape[1:], F32)
    params[0].wait()
    rate = rate_ref[...]
    dtab[1] = jnp.exp(-rate)
    etab[inner] = jnp.exp(rate * -float(ROWS))
    ftab[1] = jnp.exp(rate * -float(tok))
    ftab[2] = jnp.exp(rate * -dist.astype(F32))

    def part(h):
        return pl.ds(h * ROWS, ROWS)

    def mix(t):
        def body(m, _):
            for half in range(MIX // 2):
                n = MIX * m + 2 * half
                rows = pl.ds(pl.multiple_of(n * ROWS, 2 * ROWS), 2 * ROWS)
                masks = [ltab[which_ref[n + i]] for i in range(2)]
                for c in range(t * per, (t + 1) * per):
                    u = k_ref[rows, lane(c)].astype(F32) * v_ref[rows, lane(c)].astype(F32)
                    u_ref[c, rows, :] = u
                    for i in range(2):
                        at = pl.ds(pl.multiple_of((n + i) * ROWS, ROWS), ROWS)
                        um_all[t][c - t * per, at, :] = u[i * ROWS : (i + 1) * ROWS] * masks[i]
            return 0

        lax.fori_loop(0, chunks // MIX, body, 0)

    def scan(t):
        pairs = [(c, h) for c in range(t * per, (t + 1) * per) for h in range(halves)]

        def body(m, state):
            state = list(state)
            for i in range(SCAN):
                n = SCAN * m + i
                base = n * ROWS
                keep = which_ref[n]
                for x, (c, h) in enumerate(pairs):
                    s_all[t][c - t * per, n, part(h), :] = state[x]
                local = [None] * len(pairs)
                for j in range(ROWS):
                    rows = {
                        c: bcast(um_all[t][c - t * per, pl.ds(base + j, 1), :])
                        for c in range(t * per, (t + 1) * per)
                    }
                    for x, (c, h) in enumerate(pairs):
                        if j == 0:
                            local[x] = rows[c]
                        else:
                            local[x] = dtab[1, part(h), lane(c)] * local[x] + rows[c]
                for x, (c, h) in enumerate(pairs):
                    state[x] = etab[keep, part(h), lane(c)] * state[x] + local[x]
            return tuple(state)

        zero = jnp.zeros((ROWS, LANES), F32)
        steps = chunks // SCAN
        state = lax.fori_loop(0, steps // 2, body, tuple(zero for _ in pairs))
        serve("half", t)
        state = lax.fori_loop(steps // 2, steps, body, state)
        for x, (c, h) in enumerate(pairs):
            s_all[t][c - t * per, chunks, part(h), :] = state[x]
            tbuf[count, part(h), lane(c)] = state[x] * ftab[2, part(h), lane(c)]

            @pl.when(me == 0)
            def _():
                passed[part(h), lane(c)] = state[x]

    for r in range(count - 1):
        end = jnp.clip(final[r], 0, tok - 1)
        n = lax.shift_right_logical(end, 3)
        stop = end - n * ROWS
        b = begin[r] - n * ROWS
        where_ref[r] = n
        for j in range(ROWS):
            kind = jnp.where(j > stop, 2, jnp.where(j <= b, 0, 1))
            kind_ref[r, j] = jnp.where(ends_here[r], kind, 0)
            inside = ends_here[r] & (j >= b) & (j <= stop)
            inside_ref[r, j] = jnp.where(inside, 1.0, 0.0).astype(F32)

    def tails(t):
        for r in range(count - 1):
            n = where_ref[r]
            kinds = [kind_ref[r, j] for j in range(ROWS)]
            weights = [inside_ref[r, j] for j in range(ROWS)]
            for c in range(t * per, (t + 1) * per):
                value = [s_all[t][c - t * per, n, part(h), :] for h in range(halves)]
                for j in range(ROWS):
                    row = bcast(u_ref[c, pl.ds(n * ROWS + j, 1), :]) * weights[j]
                    value = [
                        dtab[kinds[j], part(h), lane(c)] * x + row for h, x in enumerate(value)
                    ]
                for h in range(halves):
                    tbuf[r, part(h), lane(c)] = value[h]

    def span(t):
        return pl.ds(t * width, width)

    def pass_on(t):
        return pltpu.make_async_remote_copy(
            src_ref=passed.at[:, span(t)], dst_ref=arrived.at[:, span(t)],
            send_sem=st_send.at[t], recv_sem=st_recv.at[t],
            device_id={"ctx": me + 1}, device_id_type=MESH,
        )

    def arrival(t):
        return pltpu.make_async_remote_copy(
            src_ref=passed.at[:, span(t)], dst_ref=arrived.at[:, span(t)],
            send_sem=st_send.at[t], recv_sem=st_recv.at[t],
            device_id={"ctx": me - 1}, device_id_type=MESH,
        )

    def relay(t):
        arrival(t).wait_recv()

        @pl.when(me < last)
        def _():
            for c in range(t * per, (t + 1) * per):
                for h in range(halves):
                    passed[part(h), lane(c)] = (
                        s_all[t][c - t * per, chunks, part(h), :]
                        + ftab[covers, part(h), lane(c)] * arrived[part(h), lane(c)]
                    )
            pass_on(t).start()

    def to_right(i, t):
        return pltpu.make_async_remote_copy(
            src_ref=put_r.at[i, :, span(t)], dst_ref=arr_r.at[i, :, span(t)],
            send_sem=r_send.at[i, t], recv_sem=r_recv.at[i, t],
            device_id={"ctx": me + 1}, device_id_type=MESH,
        )

    def to_left(gap, t):
        return pltpu.make_async_remote_copy(
            src_ref=put_l.at[gap - 1, :, span(t)], dst_ref=arr_l.at[gap - 1, :, span(t)],
            send_sem=l_send.at[gap - 1, t], recv_sem=l_recv.at[gap - 1, t],
            device_id={"ctx": me - gap}, device_id_type=MESH,
        )

    def give_left(t):
        for gap in range(last, 0, -1):

            @pl.when(me >= gap)
            def _():
                put_l[gap - 1, :, span(t)] = tbuf[source_of(me - gap), :, span(t)]
                to_left(gap, t).start()

    def hop(m, i, t):
        at = span(t)

        @pl.when(me == m)
        def _():
            own = tbuf[source_of(m + last - i), :, at]
            if m:
                to_right(i - 1, t).wait_recv()
                own = own + arr_r[i - 1, :, at]
            put_r[i, :, at] = own
            to_right(i, t).start()

    hops = last
    group = 2 if per % 2 == 0 else 1
    names, clock, now = [], {}, START
    for t in range(tiles):
        for name in (("half", t), ("scan", t)):
            now += SCAN_US * per / 2
            names.append(name)
            clock[name] = now
    for g in range(cols // group):
        now += TAPS_US * group
        names.append(("taps", g))
        clock[names[-1]] = now
    for g in range(cols // group):
        if g * group % per == 0:
            names.append(("carry", g * group // per))
            clock[names[-1]] = now
            now += CARRY_US * per
        now += EMIT_US * group if g * group < cols - late else 0.0
        names.append(("emit", g))
        clock[names[-1]] = now
    jobs = {name: [] for name in names}
    send_us = LINK_US * per * poles
    free, reach, open_jobs = [0.0] * slots, {}, []
    for t in range(tiles):
        open_jobs += [("relay", m, 0, t) for m in range(1, slots)]
        open_jobs += [("hop", m, i, t) for i in range(hops) for m in range(i + 1)]
    open_jobs.sort(key=lambda job: (job[0] == "hop", job[2], job[3]))

    def ship(m, now):
        free[m] = max(free[m], now) + send_us
        return free[m] + WIRE_US

    scanned = set()
    for name in names:
        now = clock[name]
        later = min([clock[x] for x in names if clock[x] > now] or [now]) + QUEUE_US
        if name[0] == "scan":
            scanned.add(name[1])
            reach["relay", 1, 0, name[1]] = ship(0, now)
        for job in list(open_jobs):
            kind, m, i, t = job
            if t not in scanned:
                continue
            if kind == "relay":
                ready = reach.get(job, 1e9) <= now and m < last
                ready = ready or name == ("carry", t)
            else:
                ready = (m == 0 or reach.get(("hop", m, i, t), 1e9) <= now)
                ready = ready and free[m] <= later
            if ready:
                jobs[name].append(job)
                open_jobs.remove(job)
                if m < last:
                    after = (kind, m + 1, i + 1 if kind == "hop" else 0, t)
                    reach[after] = ship(m, now)
    open_jobs.sort(key=lambda job: job[2])

    def run(job):
        kind, m, i, t = job
        if kind == "hop":
            hop(m, i, t)
        else:

            @pl.when(me == m)
            def _():
                relay(t)

    def serve(*name):
        for job in jobs[name]:
            run(job)

    def taps(t, c):
        at = lane(c)
        steps = (iota + 1).astype(F32)
        total = jnp.zeros((ROWS, LANES), F32)
        head = bcast(gain_ref[0:1, at])
        for p in range(poles):
            scale = bcast(cs_ref[pl.ds(p, 1), at])
            value = scale * jnp.exp(bcast(rate_ref[pl.ds(p, 1), at]) * -steps)
            w_all[t][c - t * per, p] = value
            total = total + value
            head = head + scale
        lead = jnp.where(iota == 0, head, pltpu.roll(total, 1, 0))
        taps = [lead] + [
            jnp.where(iota >= j, pltpu.roll(lead, j, 0), 0.0) for j in range(1, ROWS)
        ]
        for x, a in enumerate(starts):
            base = lax.shift_right_logical(jnp.clip(a, 0, tok - 1), 3) * ROWS
            value = jnp.zeros((ROWS, LANES), F32)
            for j in range(ROWS - 1):
                cut = jnp.int32(ROWS)
                for other in starts:
                    rel = other - base
                    cut = jnp.minimum(cut, jnp.where(rel > j, rel, ROWS))
                row = bcast(u_ref[c, pl.ds(base + j, 1), :])
                value = value - jnp.where(iota >= cut, taps[j], 0.0) * row
            fix_ref[x] = value

        def body(m, _):
            for i in range(FIR):
                n = m * FIR + i
                acc = [fix_ref[which_ref[n]], None]
                for j in range(ROWS):
                    term = taps[j] * bcast(u_ref[c, pl.ds(n * ROWS + j, 1), :])
                    acc[j % 2] = term if acc[j % 2] is None else acc[j % 2] + term
                um_all[t][c - t * per, pl.ds(pl.multiple_of(n * ROWS, ROWS), ROWS), :] = acc[0] + acc[1]
            return 0

        lax.fori_loop(0, chunks // FIR, body, 0)

    def carry(t):
        pairs = [(c, h) for c in range(t * per, (t + 1) * per) for h in range(halves)]

        def body(m, state):
            state = list(state)
            for i in range(CARRY):
                n = m * CARRY + i
                keep = which_ref[n]
                for x, (c, h) in enumerate(pairs):
                    s_all[t][c - t * per, n, part(h), :] = s_all[t][c - t * per, n, part(h), :] + state[x]
                    state[x] = etab[keep, part(h), lane(c)] * state[x]
            return tuple(state)

        lax.fori_loop(
            0, chunks // CARRY, body, tuple(arrived[part(h), lane(c)] for c, h in pairs)
        )

    def emit(t, c):
        local = c - t * per
        produce(
            lambda n: mtab[which_ref[n]], w_all[t].at[local], s_all[t].at[local],
            um_all[t].at[local], q_ref, out_ref, lane(c), poles, chunks,
        )

    for t in range(tiles):
        for copy in loads[t]:
            copy.wait()
        mix(t)
        scan(t)
        if t == 0:
            pl.semaphore_wait(barrier, last)

        @pl.when((me == 0) & (me < last))
        def _():
            pass_on(t).start()

        tails(t)
        give_left(t)
        serve("scan", t)

    params[1].wait()
    params[2].wait()
    cs_ref[...] = res_ref[...] * jnp.sqrt(1.0 - jnp.exp(-2.0 * rate_ref[...]))

    def each(step, g):
        def one(c, _):
            step(g * group // per, c)
            return 0

        lax.fori_loop(g * group, (g + 1) * group, one, 0)

    for g in range(cols // group):
        each(taps, g)
        serve("taps", g)
    for copy in q_loads:
        copy.wait()
    for g in range(cols // group):
        if g * group % per == 0:
            t = g * group // per
            serve("carry", t)

            @pl.when(me > 0)
            def _():
                carry(t)

        if g * group < made:
            each(emit, g)
        serve("emit", g)

    for job in open_jobs:
        run(job)

    dec_ref[0] = tbuf[source_of(me), :, :]
    for t in range(tiles):
        at = span(t)

        @pl.when(me > 0)
        def _():
            to_right(hops - 1, t).wait_recv()
            dec_ref[0, :, at] = dec_ref[0, :, at] + arr_r[hops - 1, :, at]

        for gap in range(1, slots):

            @pl.when(me + gap <= last)
            def _():
                to_left(gap, t).wait_recv()
                dec_ref[0, :, at] = dec_ref[0, :, at] + arr_l[gap - 1, :, at]

    for t in range(tiles):

        @pl.when(me < last)
        def _():
            pass_on(t).wait_send()

        for i in range(hops):

            @pl.when((me <= i) & (me < last))
            def _():
                to_right(i, t).wait_send()

            @pl.when(me > i)
            def _():
                to_left(i + 1, t).wait_send()


def shards(q_feat, k_feat, v_feat, pole_rate, residue, skip_gain, lengths, owners):
    tok, channels = q_feat.shape
    poles, count = pole_rate.shape[0], lengths.shape[0]
    slots = lax.axis_size("ctx")
    cols = channels // LANES
    per = min(4, cols)
    tiles = cols // per
    chunks = tok // ROWS
    hops = max(slots - 1, 1)
    dma = pltpu.SemaphoreType.DMA
    vmem, hbm = pl.BlockSpec(memory_space=pltpu.VMEM), pl.BlockSpec(memory_space=pltpu.HBM)
    ahead = tiles - 1
    late = max(per // 2, 1)
    made = cols - late
    edge = made * LANES
    state = pltpu.VMEM((poles, channels), F32)
    small = pltpu.VMEM((count, ROWS, LANES), F32)
    block = pltpu.VMEM((hops, poles, channels), F32)
    feat = pltpu.VMEM((tok, channels), q_feat.dtype)
    s_shape, near_shape = (per, chunks + 1, poles, LANES), (per, tok, LANES)
    w_shape = (per, poles, ROWS, LANES)
    handed = [
        jax.ShapeDtypeStruct((1, poles, channels), F32),
        jax.ShapeDtypeStruct(s_shape, F32),
        jax.ShapeDtypeStruct(near_shape, F32),
        jax.ShapeDtypeStruct(w_shape, F32),
        jax.ShapeDtypeStruct((tok, late * LANES), q_feat.dtype),
        jax.ShapeDtypeStruct((chunks, ROWS, LANES), F32),
    ]
    early = []
    if made:
        handed.append(jax.ShapeDtypeStruct((tok, edge), q_feat.dtype))
        early = [pltpu.VMEM((tok, edge), q_feat.dtype)]
    args = [
        pltpu.with_memory_space_constraint(x, pltpu.HBM)
        for x in (
            lengths, owners, pole_rate, residue, skip_gain[None, :], k_feat, v_feat, q_feat
        )
    ]
    handed = pl.pallas_call(
        functools.partial(kernel, tok=tok, poles=poles, count=count, cols=cols, per=per, late=late),
        in_specs=[hbm] * 8,
        out_specs=[vmem] * len(handed),
        out_shape=handed,
        scratch_shapes=early
        + [pltpu.VMEM(s_shape, F32)] * ahead
        + [pltpu.VMEM(near_shape, F32)] * ahead
        + [pltpu.VMEM(w_shape, F32)] * ahead
        + [
            pltpu.SMEM((count,), jnp.int32), pltpu.SMEM((count,), jnp.int32),
            feat, feat, state, state, pltpu.VMEM((1, channels), F32),
            pltpu.VMEM((cols, tok, LANES), F32),
            pltpu.VMEM((3, poles, channels), F32),
            pltpu.VMEM((count, poles, channels), F32),
            pltpu.VMEM((3, poles, channels), F32),
            state,
            small, small, small,
            pltpu.VMEM((count + 2, poles, channels), F32),
            state, state, block, block, block, block,
            pltpu.SMEM((chunks,), jnp.int32), pltpu.SMEM((count,), jnp.int32),
            pltpu.SMEM((count, ROWS), jnp.int32), pltpu.SMEM((count, ROWS), F32),
            dma((5,)), dma((tiles, 2)), dma((2,)), dma((tiles,)), dma((tiles,)),
            dma((hops, tiles)), dma((hops, tiles)), dma((hops, tiles)), dma((hops, tiles)),
        ],
        compiler_params=pltpu.CompilerParams(
            collective_id=0, has_side_effects=True, vmem_limit_bytes=40 << 20
        ),
        name="modal",
    )(*args)
    return pl.pallas_call(
        functools.partial(finish, poles=poles, chunks=chunks, per=per, late=late, made=made),
        in_specs=[vmem] * len(handed),
        out_specs=[hbm, hbm],
        out_shape=[
            jax.ShapeDtypeStruct((tok, channels), q_feat.dtype),
            jax.ShapeDtypeStruct((1, poles, channels), F32),
        ],
        scratch_shapes=[pltpu.VMEM((tok, late * LANES), q_feat.dtype), dma((2 + late,))],
        compiler_params=pltpu.CompilerParams(vmem_limit_bytes=8 << 20),
        name="tail",
    )(*handed)


def solution(mesh):
    tokens = P(("groups", "ctx"), "chan")
    return jax.shard_map(
        shards,
        mesh=mesh,
        in_specs=(
            tokens, tokens, tokens, P(None, "chan"), P(None, "chan"), P("chan"),
            P("groups"), P("groups"),
        ),
        out_specs=(tokens, P(("groups", "ctx"), None, "chan")),
        check_vma=False,
    )
```
